32 devices in a mesh: replica: 2 (over x), shard: 16 (over z, y, core).
Axes of the slice: x: 2, y: 2, z: 4, core: 2. Of those that a mesh axis runs over, the one named last changes fastest.
Arguments:
- tokens: bfloat16 [6144, 2048], P(('replica', 'shard')), may hold values from -6 to 6
- seg_ids: int32 [6144], P(('replica', 'shard')), may hold values from 0 to 23, as said below
- cotangent: bfloat16 [6144, 2048], P(('replica', 'shard')), may hold values from -6 to 6
- w_in: float32 [2048, 14336], P('shard')
- w_out: float32 [2048, 2048], P('shard'), may hold values from -0.75 to 0.75
- w_fc2: float32 [8192, 2048], P('shard'), may hold values from -0.0625 to 0.0625
- vectors: float32 [22528], P('shard')
- m_in: float32 [2048, 14336], P('shard'), may hold values from -6 to 6
- v_in: float32 [2048, 14336], P('shard'), may hold values from 0.6144 to 6.144
- m_out: float32 [2048, 2048], P('shard'), may hold values from -6 to 6
- v_out: float32 [2048, 2048], P('shard'), may hold values from 0.6144 to 6.144
- m_fc2: float32 [8192, 2048], P('shard'), may hold values from -6 to 6
- v_fc2: float32 [8192, 2048], P('shard'), may hold values from 0.6144 to 6.144
- m_vec: float32 [22528], P('shard'), may hold values from -6 to 6
- v_vec: float32 [22528], P('shard'), may hold values from 0.6144 to 6.144
Outputs:
- output: bfloat16 [6144, 2048], P(('replica', 'shard'))
- grad_tokens: float32 [6144, 2048], P(('replica', 'shard'))
- grad_in: float32 [2048, 14336], P('shard')
- grad_out: float32 [2048, 2048], P('shard')
- grad_fc2: float32 [8192, 2048], P('shard')
- grad_vec: float32 [22528], P('shard')
- new_in: float32 [2048, 14336], P('shard')
- new_out: float32 [2048, 2048], P('shard')
- new_fc2: float32 [8192, 2048], P('shard')
- new_vec: float32 [22528], P('shard')
- new_m_in: float32 [2048, 14336], P('shard')
- new_v_in: float32 [2048, 14336], P('shard')
- new_m_out: float32 [2048, 2048], P('shard')
- new_v_out: float32 [2048, 2048], P('shard')
- new_m_fc2: float32 [8192, 2048], P('shard')
- new_v_fc2: float32 [8192, 2048], P('shard')
- new_m_vec: float32 [22528], P('shard')
- new_v_vec: float32 [22528], P('shard')
The draws below stay inside these ranges and needn't reach their ends.
Inputs may be any that keep to these rules, and one draw needn't show every extreme that they name: `seg_ids`: within each device's block of 192 consecutive tokens the ids start at 0 and never fall; a run of equal ids is one sequence, so no sequence crosses a block. Some block holds a single sequence of 192 tokens, and some block holds sequences of 8 tokens each.
All inputs are finite; a program needn't handle non-finite values.
Results may differ from the reference program's by a relative error of at most 0.004.
The reference program's roundings to bfloat16 on the way count: a program that leaves them out, or rounds other values in their place, can miss the bound.
Values may be sent and summed in bfloat16 or wider, within the bound.
No kernel may reach another device: no remote copies, remote signals or barrier semaphores. Data moves between devices by JAX's collectives and lax.ppermute only.
A program may use at most 640 MiB of HBM per device.

```python
import math
import jax
import jax.numpy as jnp
from jax import lax

D = 2048
FF = 8192
HEAD = 64
ROT = 32
ADAM_STEP = 4
TOK_DEV = 192
TOKENS = 6144
NVEC = 22528


def draw_seg_ids(key, part):
    blocks = TOKENS // TOK_DEV
    most = TOK_DEV // 8 - 1
    first_key = jax.random.fold_in(key, 11)
    second_key = jax.random.fold_in(key, 12)
    third_key = jax.random.fold_in(key, 13)
    level = jax.random.randint(first_key, (blocks, 1), 0, 6)
    density = jnp.left_shift(jnp.ones_like(level), level) - 1
    single = jax.random.randint(third_key, (), 0, blocks)
    rows = jnp.arange(blocks, dtype=jnp.int32)[:, None]
    density = jnp.where(rows == single, 0, density)
    cuts = jax.random.randint(second_key, (blocks, TOK_DEV), 0, TOK_DEV) < density
    cuts = cuts & (jnp.arange(TOK_DEV, dtype=jnp.int32)[None, :] > 0)
    ids = jnp.minimum(jnp.cumsum(cuts.astype(jnp.int32), axis=1), most)
    regular = jnp.arange(TOK_DEV, dtype=jnp.int32)[None, :] // 8
    dense = (single + 1) % blocks
    ids = jnp.where(rows == dense, regular, ids)
    return ids.reshape(TOKENS).astype(jnp.int32)


def draw_w_in(key, part):
    ncols = 3 * D + FF
    base = jax.random.normal(key, (D, ncols), jnp.float32) * (1.0 / math.sqrt(D))
    return base


def draw_vectors(key, part):
    first_key = jax.random.fold_in(key, 21)
    second_key = jax.random.fold_in(key, 22)
    third_key = jax.random.fold_in(key, 23)
    biases = 0.3 * jax.random.normal(first_key, (D, 9), jnp.float32)
    gains = jax.random.uniform(second_key, (D, 1), jnp.float32, 0.6, 1.4)
    shifts = 0.3 * jax.random.normal(third_key, (D, 1), jnp.float32)
    return jnp.concatenate([biases, gains, shifts], axis=1).reshape(11 * D)


def levels(key, shape, shards, least, top_value):
    level = 1.0
    for position, blocks in shards:
        steps = jax.random.uniform(jax.random.fold_in(jax.random.fold_in(key, 6), position), (blocks,), jnp.float32, least / len(shards), top_value / len(shards))
        level = level * jnp.repeat(jnp.exp(steps), shape[position] // blocks).reshape((-1,) + (1,) * (len(shape) - 1 - position))
    return level


def normal_values(rng, extent, deviation, reach, shards=(), kind=jnp.bfloat16):
    loudness = levels(rng, extent, shards, -0.22, 0.18) if shards else 1.0
    values = jax.random.normal(rng, extent, jnp.float32) * deviation * loudness
    return jnp.minimum(jnp.maximum(values, -reach), reach).astype(kind)


def setup_inputs(seed: int = 0) -> dict:
    seeds = jax.random.split(jax.random.key(seed), 16)
    return {
        "tokens": normal_values(seeds[0], (TOKENS, D), 1.0, 6.0, ((0, 32),)),
        "seg_ids": draw_seg_ids(jax.random.fold_in(seeds[15], 71), 0),
        "cotangent": normal_values(seeds[2], (TOKENS, D), 1.0, 6.0, ((0, 32),)),
        "w_in": draw_w_in(jax.random.fold_in(seeds[15], 71), 0),
        "w_out": normal_values(seeds[4], (D, D), (D // 32) ** -0.5, 0.75, ((0, 16),), jnp.float32),
        "w_fc2": normal_values(seeds[5], (FF, D), FF ** -0.5, 0.0625, ((0, 16),), jnp.float32),
        "vectors": draw_vectors(jax.random.fold_in(seeds[15], 71), 0),
        "m_in": normal_values(seeds[7], (D, 3 * D + FF), (0.03 * TOKENS ** 0.5), 6.0, ((0, 16),), jnp.float32),
        "v_in": jnp.clip(jnp.exp(math.log(6.144) - 2.3025851 * jax.random.uniform(seeds[8], (D, 3 * D + FF), jnp.float32) ** levels(seeds[8], (D, 3 * D + FF), ((0, 16),), -0.2, 0.2)), 0.6144, 6.144),
        "m_out": normal_values(seeds[9], (D, D), (0.03 * TOKENS ** 0.5), 6.0, ((0, 16),), jnp.float32),
        "v_out": jnp.clip(jnp.exp(math.log(6.144) - 2.3025851 * jax.random.uniform(seeds[10], (D, D), jnp.float32) ** levels(seeds[10], (D, D), ((0, 16),), -0.2, 0.2)), 0.6144, 6.144),
        "m_fc2": normal_values(seeds[11], (FF, D), (0.03 * TOKENS ** 0.5), 6.0, ((0, 16),), jnp.float32),
        "v_fc2": jnp.clip(jnp.exp(math.log(6.144) - 2.3025851 * jax.random.uniform(seeds[12], (FF, D), jnp.float32) ** levels(seeds[12], (FF, D), ((0, 16),), -0.2, 0.2)), 0.6144, 6.144),
        "m_vec": normal_values(seeds[13], (NVEC,), (0.03 * TOKENS ** 0.5), 6.0, ((0, 16),), jnp.float32),
        "v_vec": jnp.clip(jnp.exp(math.log(6.144) - 2.3025851 * jax.random.uniform(seeds[14], (NVEC,), jnp.float32) ** levels(seeds[14], (NVEC,), ((0, 16),), -0.2, 0.2)), 0.6144, 6.144),
    }


NORM_EPS = 1e-05
SCORE_SCALE = 0.125
LEARN_RATE = 0.02
BETA_ONE = 0.9
BETA_TWO = 0.98
ADAM_EPS = 1e-08
DECAY = 0.1

@jax.custom_vjp
def low(v):
    return lax.optimization_barrier(v.astype(jnp.bfloat16)).astype(jnp.float32)

@jax.custom_vjp
def low_back(v):
    return v

def low_keep(v):
    return (low(v), None)

def low_pass(kept, grad):
    return (grad,)

def back_keep(v):
    return (v, None)

def back_low(kept, grad):
    return (low(grad),)
low.defvjp(low_keep, low_pass)
low_back.defvjp(back_keep, back_low)

def split_vectors(vectors):
    grouped = vectors.reshape(D, 11)
    bias_in = jnp.concatenate([grouped[:, 0], grouped[:, 1], grouped[:, 2], grouped[:, 3:7].reshape(FF)])
    return (bias_in, grouped[:, 7], grouped[:, 8], grouped[:, 9], grouped[:, 10])

def rotary_tables(seg_ids):
    length = seg_ids.shape[0]
    order = jnp.arange(length, dtype=jnp.int32)
    same = seg_ids[:, None] == seg_ids[None, :]
    earlier = same & (order[None, :] < order[:, None])
    place = lax.optimization_barrier(jnp.sum(earlier.astype(jnp.float32), axis=1))
    freqs = 10000.0 ** (-jnp.arange(ROT // 2, dtype=jnp.float32) * (2.0 / ROT))
    angles = place[:, None] * freqs[None, :]
    allowed = same & (order[None, :] <= order[:, None])
    return (jnp.cos(angles)[:, None, :], jnp.sin(angles)[:, None, :], allowed)

def rotate(values, cosine, sine):
    half = ROT // 2
    first = values[..., :half]
    second = values[..., half:ROT]
    return jnp.concatenate([first * cosine - second * sine, second * cosine + first * sine, values[..., ROT:]], axis=-1)

def attend(queries, keys, values, seg_ids):
    cosine, sine, allowed = rotary_tables(seg_ids)
    queries = low(rotate(queries, cosine, sine))
    keys = low(rotate(keys, cosine, sine))
    values = low(values)
    scores = low_back(jnp.einsum('qhd,khd->hqk', queries, keys, precision=lax.Precision.HIGHEST) * SCORE_SCALE)
    probs = jax.nn.softmax(jnp.where(allowed[None], scores, -1e+30), axis=2)
    return jnp.einsum('hqk,khd->qhd', low(probs), values, precision=lax.Precision.HIGHEST)

def adamw(weight, grad, first, second, decay):
    first = BETA_ONE * first + (1.0 - BETA_ONE) * grad
    second = BETA_TWO * second + (1.0 - BETA_TWO) * grad * grad
    first_hat = first / (1.0 - BETA_ONE ** ADAM_STEP)
    second_hat = second / (1.0 - BETA_TWO ** ADAM_STEP)
    weight = weight - LEARN_RATE * (first_hat / (jnp.sqrt(second_hat) + ADAM_EPS) + decay * weight)
    return (weight, first, second)

def reference(tokens, seg_ids, cotangent, w_in, w_out, w_fc2, vectors, m_in, v_in, m_out, v_out, m_fc2, v_fc2, m_vec, v_vec):
    heads = D // HEAD
    blocks = TOKENS // TOK_DEV
    inputs = tokens.astype(jnp.float32)
    upstream = cotangent.astype(jnp.float32)

    def forward(inputs, w_in, w_out, w_fc2, vectors):
        bias_in, bias_out, bias_fc, gain, shift = split_vectors(vectors)
        centred = inputs - lax.optimization_barrier(jnp.mean(inputs, axis=1, keepdims=True))
        standard = centred * lax.rsqrt(lax.optimization_barrier(jnp.mean(centred * centred, axis=1, keepdims=True)) + NORM_EPS)
        normed = low(standard * gain + shift)
        projected = low_back(jnp.dot(normed, low(w_in), precision=lax.Precision.HIGHEST) + bias_in)
        queries = projected[:, :D].reshape(blocks, TOK_DEV, heads, HEAD)
        keys = projected[:, D:2 * D].reshape(blocks, TOK_DEV, heads, HEAD)
        values = projected[:, 2 * D:3 * D].reshape(blocks, TOK_DEV, heads, HEAD)
        feed = projected[:, 3 * D:]
        attended = lax.map(jax.checkpoint(lambda group: attend(group[0], group[1], group[2], group[3])), (queries, keys, values, seg_ids.reshape(blocks, TOK_DEV)))
        attended = low(low_back(attended.reshape(TOKENS, D)))
        hidden = low(jax.nn.gelu(feed, approximate=True))
        branch_attn = jnp.dot(attended, low(w_out), precision=lax.Precision.HIGHEST) + bias_out
        branch_mlp = jnp.dot(hidden, low(w_fc2), precision=lax.Precision.HIGHEST) + bias_fc
        return inputs + branch_attn + branch_mlp
    result, backward = jax.vjp(forward, inputs, w_in, w_out, w_fc2, vectors)
    grad_tokens, grad_in, grad_out, grad_fc2, grad_vec = backward(upstream)
    new_in, new_m_in, new_v_in = adamw(w_in, grad_in, m_in, v_in, DECAY)
    new_out, new_m_out, new_v_out = adamw(w_out, grad_out, m_out, v_out, DECAY)
    new_fc2, new_m_fc2, new_v_fc2 = adamw(w_fc2, grad_fc2, m_fc2, v_fc2, DECAY)
    new_vec, new_m_vec, new_v_vec = adamw(vectors, grad_vec, m_vec, v_vec, 0.0)
    return (result.astype(jnp.bfloat16), grad_tokens, grad_in, grad_out, grad_fc2, grad_vec, new_in, new_out, new_fc2, new_vec, new_m_in, new_v_in, new_m_out, new_v_out, new_m_fc2, new_v_fc2, new_m_vec, new_v_vec)
```

```python
import jax
import jax.numpy as jnp
from jax import lax
from jax.experimental import pallas as pl
from jax.experimental.pallas import tpu as pltpu
from jax.sharding import PartitionSpec as P

D = 2048
FF = 8192
HEAD = 64
ROT = 32
ADAM_STEP = 4

NORM_EPS = 1e-05
SCORE_SCALE = 0.125
LEARN_RATE = 0.02
BETA_ONE = 0.9
BETA_TWO = 0.98
ADAM_EPS = 1e-08
DECAY = 0.1

RANKS = 16
NZ = 4
QCOL = D // RANKS
FCOL = FF // RANKS
PROJ = 3 * QCOL + FCOL
PAIR = QCOL + FCOL
LOW = jnp.bfloat16
F32 = jnp.float32
BY_LAST = (((1,), (1,)), ((), ()))
BY_FIRST = (((0,), (0,)), ((), ()))


def adamw(weight, grad, first, second, decay):
    first = BETA_ONE * first + (1.0 - BETA_ONE) * grad
    second = BETA_TWO * second + (1.0 - BETA_TWO) * grad * grad
    first_hat = first / (1.0 - BETA_ONE**ADAM_STEP)
    second_hat = second / (1.0 - BETA_TWO**ADAM_STEP)
    weight = weight - LEARN_RATE * (first_hat / (jnp.sqrt(second_hat) + ADAM_EPS) + decay * weight)
    return (weight, first, second)


def dot(a, b, dims=(((1,), (0,)), ((), ()))):
    return lax.dot_general(a, b, dims, preferred_element_type=F32)


def middle_kernel(
    proj_ref, gh_ref, bias_ref, cos_ref, sin_ref, segc_ref, segr_ref, ah_ref, gp_ref, sum_ref
):
    length = proj_ref.shape[0]
    half = ROT // 2
    lane = lax.broadcasted_iota(jnp.int32, (length, QCOL), 1)
    inner = lane % HEAD
    cosine = cos_ref[...]
    sine = sin_ref[...]
    sin_low = jnp.where(inner < half, sine, 0.0)
    sin_high = jnp.where(inner >= half, sine, 0.0)

    def turn(x):
        return (
            x * cosine
            - pltpu.roll(x, QCOL - half, 1) * sin_low
            + pltpu.roll(x, half, 1) * sin_high
        )

    def turn_back(x):
        return (
            x * cosine
            + pltpu.roll(x, QCOL - half, 1) * sin_low
            - pltpu.roll(x, half, 1) * sin_high
        )

    bias = bias_ref[...]
    q = turn(proj_ref[:, :QCOL] + bias[:, :QCOL]).astype(LOW)
    k = turn(proj_ref[:, QCOL : 2 * QCOL] + bias[:, QCOL : 2 * QCOL]).astype(LOW)
    v = (proj_ref[:, 2 * QCOL : 3 * QCOL] + bias[:, 2 * QCOL : 3 * QCOL]).astype(LOW)
    ga = gh_ref[:, :QCOL].astype(LOW)
    row = lax.broadcasted_iota(jnp.int32, (length, length), 0)
    col = lax.broadcasted_iota(jnp.int32, (length, length), 1)
    allowed = (segc_ref[...] == segr_ref[0]) & (col <= row)
    zero = jnp.zeros((length, QCOL), LOW)
    attended = jnp.zeros((length, QCOL), F32)
    dq = jnp.zeros((length, QCOL), F32)
    dk = jnp.zeros((length, QCOL), F32)
    dv = jnp.zeros((length, QCOL), F32)
    for head in range(QCOL // HEAD):
        mine = (lane >= head * HEAD) & (lane < (head + 1) * HEAD)
        qh = jnp.where(mine, q, zero)
        kh = jnp.where(mine, k, zero)
        vh = jnp.where(mine, v, zero)
        gah = jnp.where(mine, ga, zero)
        scores = jnp.where(allowed, dot(qh, k, BY_LAST) * SCORE_SCALE, -1e30)
        peak = jnp.max(scores, axis=1, keepdims=True)
        grown = jnp.exp(scores - peak)
        probs = grown / jnp.sum(grown, axis=1, keepdims=True)
        low = probs.astype(LOW)
        attended = attended + dot(low, vh)
        dp = dot(gah, v, BY_LAST)
        dv = dv + dot(low, gah, BY_FIRST)
        ds = (probs * (dp - jnp.sum(probs * dp, axis=1, keepdims=True))).astype(LOW)
        dq = dq + dot(ds, kh)
        dk = dk + dot(ds, qh, BY_FIRST)
    ah_ref[:, :QCOL] = attended.astype(LOW)
    dq = turn_back(dq * SCORE_SCALE).astype(LOW)
    dk = turn_back(dk * SCORE_SCALE).astype(LOW)
    dv = dv.astype(LOW)
    u = proj_ref[:, 3 * QCOL :] + bias[:, 3 * QCOL :]
    c0 = 0.7978845608028654
    c1 = 0.044715
    square = u * u
    bent = jnp.tanh(c0 * (u + c1 * square * u))
    lift = 0.5 * (1.0 + bent)
    ah_ref[:, QCOL:] = (u * lift).astype(LOW)
    slope = lift + 0.5 * u * (1.0 - bent * bent) * (c0 * (1.0 + 3.0 * c1 * square))
    df = (gh_ref[:, QCOL:] * slope).astype(LOW)
    gp_ref[:, :QCOL] = dq
    gp_ref[:, QCOL : 2 * QCOL] = dk
    gp_ref[:, 2 * QCOL : 3 * QCOL] = dv
    gp_ref[:, 3 * QCOL :] = df

    @pl.when(pl.program_id(0) == 0)
    def _():
        sum_ref[...] = jnp.zeros_like(sum_ref)

    for at, part in ((0, dq), (QCOL, dk), (2 * QCOL, dv), (3 * QCOL, df)):
        width = part.shape[1]
        sum_ref[:, at : at + width] += jnp.sum(part.astype(F32), axis=0, keepdims=True)


def middle(proj, gh, bias, cosine, sine, segc, segr):
    rows = proj.shape[0]
    blocks = segr.shape[0]
    length = rows // blocks

    def tall(width):
        return pl.BlockSpec((length, width), lambda i: (i, 0))

    def still(shape):
        return pl.BlockSpec(shape, lambda i: (0, 0))

    return pl.pallas_call(
        middle_kernel,
        grid=(blocks,),
        in_specs=[
            tall(PROJ),
            tall(PAIR),
            still((1, PROJ)),
            tall(QCOL),
            tall(QCOL),
            tall(1),
            pl.BlockSpec((1, 1, length), lambda i: (i, 0, 0)),
        ],
        out_specs=[tall(PAIR), tall(PROJ), still((1, PROJ))],
        out_shape=[
            jax.ShapeDtypeStruct((rows, PAIR), LOW),
            jax.ShapeDtypeStruct((rows, PROJ), LOW),
            jax.ShapeDtypeStruct((1, PROJ), F32),
        ],
        compiler_params=pltpu.CompilerParams(dimension_semantics=("arbitrary",)),
        cost_estimate=pl.CostEstimate(
            flops=14 * rows * length * QCOL + 60 * rows * PROJ,
            bytes_accessed=rows * (6 * PROJ + 6 * PAIR + 8 * QCOL),
            transcendentals=rows * (2 * length + FCOL),
        ),
        name="middle",
    )(proj, gh, bias, cosine, sine, segc, segr)


def make_on_device(mesh):
    shards = mesh.shape["shard"]
    copies = mesh.shape["replica"]
    fold = shards // RANKS
    rank_of = lambda z, y, c: (z * 2 + y) * 2 + c

    def moves(target):
        pairs = []
        for z in range(NZ):
            for y in range(2):
                for c in range(2):
                    to = rank_of(*target(z, y, c))
                    for f in range(fold):
                        pairs.append((rank_of(z, y, c) * fold + f, to * fold + f))
        return pairs

    swap_core = moves(lambda z, y, c: (z, y, 1 - c))
    swap_y = moves(lambda z, y, c: (z, 1 - y, c))
    up_z = [moves(lambda z, y, c, n=n: ((z + n) % NZ, y, c)) for n in range(NZ)]

    def core(x):
        return lax.ppermute(x, "shard", swap_core)

    def across_y(x):
        return lax.ppermute(x, "shard", swap_y)

    def along_z(x, n):
        return lax.ppermute(x, "shard", up_z[n % NZ])

    def across_fold(x, n):
        return lax.ppermute(
            x,
            "shard",
            [(r * fold + f, r * fold + (f + n) % fold) for r in range(RANKS) for f in range(fold)],
        )

    def next_copy(x, n):
        return lax.ppermute(x, "replica", [(i, (i + n) % copies) for i in range(copies)])

    def fold_gather(x, f):
        if fold == 1:
            return x
        parts = jnp.stack([x] + [across_fold(x, n) for n in range(1, fold)])
        order = (f - jnp.arange(fold)) % fold
        return jnp.take(parts, order, axis=0).reshape((fold * x.shape[0],) + x.shape[1:])

    def fold_scatter(x, f):
        if fold == 1:
            return x
        parts = x.reshape((fold, x.shape[0] // fold) + x.shape[1:])
        total = lax.dynamic_index_in_dim(parts, f, 0, keepdims=False)
        for n in range(1, fold):
            part = lax.dynamic_index_in_dim(parts, (f + n) % fold, 0, keepdims=False)
            total = total + across_fold(part, n).astype(F32)
        return total

    def gather_z(x):
        chunks = []
        for n in range(NZ):
            if n:
                x = along_z(x, 1)
            two = jnp.concatenate([x, across_y(x)], axis=0)
            chunks.append(jnp.concatenate([two, core(two)], axis=0))
        return chunks

    def on_device(
        tokens,
        seg_ids,
        cotangent,
        w_in,
        w_out,
        w_fc2,
        vectors,
        m_in,
        v_in,
        m_out,
        v_out,
        m_fc2,
        v_fc2,
        m_vec,
        v_vec,
    ):
        length = tokens.shape[0]
        owned = w_in.shape[0]
        me = lax.axis_index("shard")
        copy = lax.axis_index("replica")
        t = me // fold
        f = me % fold
        z, y, c = t // 4, (t // 2) % 2, t % 2

        g_chunks = gather_z(cotangent)

        low_in = fold_gather(w_in.astype(LOW), f)
        rows = low_in.shape[0]
        part = rows // copies
        low_in = low_in.reshape(copies, part, -1)
        low_in = lax.dynamic_index_in_dim(low_in, copy, 0, keepdims=False)
        by_rank = jnp.concatenate(
            [
                low_in[:, :D].reshape(part, RANKS, QCOL),
                low_in[:, D : 2 * D].reshape(part, RANKS, QCOL),
                low_in[:, 2 * D : 3 * D].reshape(part, RANKS, QCOL),
                low_in[:, 3 * D :].reshape(part, RANKS, FCOL),
            ],
            axis=2,
        )
        turned = by_rank.transpose(1, 0, 2).reshape(NZ, 2, 2, part, PROJ)
        kept = lax.dynamic_index_in_dim(turned, c, 2, keepdims=False)
        came = core(lax.dynamic_index_in_dim(turned, 1 - c, 2, keepdims=False))
        turned = jnp.stack([jnp.where(c == 0, kept, came), jnp.where(c == 0, came, kept)], axis=2)
        kept = lax.dynamic_index_in_dim(turned, y, 1, keepdims=False)
        came = across_y(lax.dynamic_index_in_dim(turned, 1 - y, 1, keepdims=False))
        turned = jnp.stack([jnp.where(y == 0, kept, came), jnp.where(y == 0, came, kept)], axis=1)
        by_z = [lax.dynamic_index_in_dim(turned, z, 0, keepdims=False)]
        for n in range(1, NZ):
            by_z.append(
                along_z(lax.dynamic_index_in_dim(turned, (z + n) % NZ, 0, keepdims=False), n)
            )
        mine = jnp.stack(by_z, axis=0)
        mine = jnp.take(mine, (z - jnp.arange(NZ)) % NZ, axis=0).reshape(RANKS, part, PROJ)
        if copies > 1:
            both = jnp.stack([mine] + [next_copy(mine, n) for n in range(1, copies)], axis=1)
            both = jnp.take(both, (copy - jnp.arange(copies)) % copies, axis=1)
        else:
            both = mine[:, None]
        w_cols = both.reshape(D, PROJ)
        w_pair = jnp.concatenate(
            [fold_gather(w_out.astype(LOW), f), fold_gather(w_fc2.astype(LOW), f)], axis=0
        )

        order = jnp.arange(length, dtype=jnp.int32)
        same = seg_ids[:, None] == seg_ids[None, :]
        place = jnp.sum((same & (order[None, :] < order[:, None])).astype(F32), axis=1)
        grouped = fold_gather(vectors.reshape(-1, 11), f)
        small = jnp.concatenate([grouped[:, 9], grouped[:, 10], seg_ids.astype(F32), place])
        small = small.reshape(1, -1)
        small = jnp.concatenate([small] + [along_z(small, n) for n in range(1, NZ)], axis=0)
        small = jnp.stack([small, across_y(small)], axis=1)
        small = jnp.stack([small, core(small)], axis=2)
        width = small.shape[-1]
        gains = small[..., : 2 * QCOL]
        gains = jnp.take(gains, (z - jnp.arange(NZ)) % NZ, axis=0)
        gains = jnp.where(y == 0, gains, gains[:, ::-1])
        gains = jnp.where(c == 0, gains, gains[:, :, ::-1]).reshape(RANKS, 2, QCOL)
        gain = gains[:, 0].reshape(D)
        shift = gains[:, 1].reshape(D)
        tail = small[..., 2 * QCOL :].transpose(0, 2, 1, 3).reshape(NZ, 4, 2, length)
        segs = tail[:, :, 0]
        places = tail[:, :, 1]
        lane = jnp.arange(QCOL, dtype=jnp.int32) % HEAD
        freqs = 10000.0 ** (-(lane % (ROT // 2)).astype(F32) * (2.0 / ROT))
        freqs = jnp.where(lane < ROT, freqs, 0.0)
        angles = places.reshape(NZ, 4 * length, 1) * freqs
        cosine = jnp.cos(angles)
        sine = jnp.sin(angles)

        inputs = tokens.astype(F32)
        centred = inputs - jnp.mean(inputs, axis=1, keepdims=True)
        inv_std = lax.rsqrt(jnp.mean(centred * centred, axis=1, keepdims=True) + NORM_EPS)
        standard = centred * inv_std
        normed = (standard * gain + shift).astype(LOW)
        n_chunks = gather_z(normed)

        bias_in = jnp.concatenate(
            [grouped[:, 0], grouped[:, 1], grouped[:, 2], grouped[:, 3:7].reshape(FCOL)]
        ).reshape(1, PROJ)
        bias_tail = lax.dynamic_update_slice(
            jnp.zeros((D,), F32), grouped[:, 7] + grouped[:, 8], (t * QCOL,)
        )

        def scatter_add(left, right, dims, n, extra=None):
            near = dot(left[: 2 * length], right, dims)
            far = dot(left[2 * length :], right, dims)
            if extra is not None:
                near = near + extra
                far = far + extra
            near = near + core(far.astype(LOW)).astype(F32)
            own = near[:length] + across_y(near[length:].astype(LOW)).astype(F32)
            if n == 0:
                return own
            return along_z(own.astype(LOW), -n).astype(F32)

        out_total = None
        gn_total = None
        grad_in = None
        grad_pair = None
        proj_sum = None
        for n in range(NZ):
            gc = g_chunks[n]
            nc = n_chunks[n]
            gh = dot(gc, w_pair, BY_LAST)
            proj = dot(nc, w_cols)
            ah, gp, sums = middle(
                proj,
                gh,
                bias_in,
                cosine[n],
                sine[n],
                segs[n].reshape(4 * length, 1),
                segs[n].reshape(4, 1, length),
            )
            part_in = dot(nc, gp, BY_FIRST)
            part_pair = dot(ah, gc, BY_FIRST)
            part_out = scatter_add(ah, w_pair, (((1,), (0,)), ((), ())), n, bias_tail)
            part_gn = scatter_add(gp, w_cols, BY_LAST, n)
            if n == 0:
                grad_in, grad_pair, proj_sum = part_in, part_pair, sums
                out_total, gn_total = part_out, part_gn
            else:
                grad_in = grad_in + part_in
                grad_pair = grad_pair + part_pair
                proj_sum = proj_sum + sums
                out_total = out_total + part_out
                gn_total = gn_total + part_gn

        output = (inputs + out_total).astype(LOW)
        upstream = cotangent.astype(F32)
        scaled = gn_total * gain
        grad_tokens = upstream + inv_std * (
            scaled
            - jnp.mean(scaled, axis=1, keepdims=True)
            - standard * jnp.mean(scaled * standard, axis=1, keepdims=True)
        )

        sums = jnp.stack(
            [jnp.sum(upstream, axis=0), jnp.sum(gn_total * standard, axis=0), jnp.sum(gn_total, axis=0)]
        )
        sums = sums + core(sums)
        sums = sums + across_y(sums)
        for moved in [along_z(sums, n) for n in range(1, NZ)]:
            sums = sums + moved
        sums = lax.dynamic_slice(sums, (0, t * QCOL), (3, QCOL))
        vec = jnp.concatenate(
            [
                proj_sum[0, : 3 * QCOL].reshape(3, QCOL).T,
                proj_sum[0, 3 * QCOL :].reshape(QCOL, 4),
                sums[0][:, None],
                sums[0][:, None],
                sums[1][:, None],
                sums[2][:, None],
            ],
            axis=1,
        )
        vec = fold_scatter(vec, f).reshape(-1)
        for moved in [next_copy(vec, n) for n in range(1, copies)]:
            vec = vec + moved

        g_out = fold_scatter(grad_pair[:QCOL], f)
        g_fc2 = fold_scatter(grad_pair[QCOL:], f)
        g_pair = jnp.concatenate([g_out, g_fc2], axis=0).astype(LOW)
        pair_total = g_pair.astype(F32)
        for n in range(1, copies):
            pair_total = pair_total + next_copy(g_pair, n).astype(F32)
        grad_out = pair_total[: g_out.shape[0]]
        grad_fc2 = pair_total[g_out.shape[0] :]

        grad_in = grad_in.reshape(RANKS, copies, part, PROJ)
        total = lax.dynamic_index_in_dim(grad_in, copy, 1, keepdims=False)
        for n in range(1, copies):
            sent = lax.dynamic_index_in_dim(grad_in, (copy + n) % copies, 1, keepdims=False)
            total = total + next_copy(sent.astype(LOW), n).astype(F32)
        back = total.astype(LOW).reshape(NZ, 2, 2, part, PROJ)
        by_z = [lax.dynamic_index_in_dim(back, z, 0, keepdims=False)]
        for n in range(1, NZ):
            by_z.append(along_z(lax.dynamic_index_in_dim(back, (z + n) % NZ, 0, keepdims=False), n))
        back = jnp.take(jnp.stack(by_z), (z - jnp.arange(NZ)) % NZ, axis=0)
        kept = lax.dynamic_index_in_dim(back, y, 1, keepdims=False)
        came = across_y(lax.dynamic_index_in_dim(back, 1 - y, 1, keepdims=False))
        back = jnp.stack([jnp.where(y == 0, kept, came), jnp.where(y == 0, came, kept)], axis=1)
        kept = lax.dynamic_index_in_dim(back, c, 2, keepdims=False)
        came = core(lax.dynamic_index_in_dim(back, 1 - c, 2, keepdims=False))
        back = jnp.stack([jnp.where(c == 0, kept, came), jnp.where(c == 0, came, kept)], axis=2)
        back = back.reshape(RANKS, part, PROJ)
        if copies > 1:
            both = jnp.stack([back] + [next_copy(back, n) for n in range(1, copies)], axis=1)
            both = jnp.take(both, (copy - jnp.arange(copies)) % copies, axis=1)
        else:
            both = back[:, None]
        both = both.reshape(RANKS, rows, PROJ).transpose(1, 0, 2)
        both = jnp.concatenate(
            [
                both[:, :, :QCOL].reshape(rows, D),
                both[:, :, QCOL : 2 * QCOL].reshape(rows, D),
                both[:, :, 2 * QCOL : 3 * QCOL].reshape(rows, D),
                both[:, :, 3 * QCOL :].reshape(rows, FF),
            ],
            axis=1,
        )
        grad_w_in = fold_scatter(both, f).astype(F32)

        new_in, new_m_in, new_v_in = adamw(w_in, grad_w_in, m_in, v_in, DECAY)
        new_out, new_m_out, new_v_out = adamw(w_out, grad_out, m_out, v_out, DECAY)
        new_fc2, new_m_fc2, new_v_fc2 = adamw(w_fc2, grad_fc2, m_fc2, v_fc2, DECAY)
        new_vec, new_m_vec, new_v_vec = adamw(vectors, vec, m_vec, v_vec, 0.0)
        return (
            output,
            grad_tokens,
            grad_w_in,
            grad_out,
            grad_fc2,
            vec,
            new_in,
            new_out,
            new_fc2,
            new_vec,
            new_m_in,
            new_v_in,
            new_m_out,
            new_v_out,
            new_m_fc2,
            new_v_fc2,
            new_m_vec,
            new_v_vec,
        )

    return on_device


def solution(mesh):
    both = P(("replica", "shard"), None)
    flat = P("shard")
    rows = P("shard", None)
    return jax.shard_map(
        make_on_device(mesh),
        mesh=mesh,
        in_specs=(both, P(("replica", "shard")), both, rows, rows, rows, flat)
        + (rows,) * 6
        + (flat, flat),
        out_specs=(both, both, rows, rows, rows, flat)
        + (rows, rows, rows, flat)
        + (rows,) * 6
        + (flat, flat),
        check_vma=False,
    )
```

```python
import jax
import jax.numpy as jnp
from jax import lax
from jax.experimental import pallas as pl
from jax.experimental.pallas import tpu as pltpu
from jax.sharding import PartitionSpec as P


D = 2048
FF = 8192
HEAD = 64
ROT = 32
ADAM_STEP = 4

NORM_EPS = 1e-05
SCORE_SCALE = 0.125
LEARN_RATE = 0.02
BETA_ONE = 0.9
BETA_TWO = 0.98
ADAM_EPS = 1e-08
DECAY = 0.1

RANKS = 16
NZ = 4
CHUNKS = (0, 3, 2, 1)
GRAD_ORDER = (2, 3, 1, 0)
EARLY = 2
QCOL = D // RANKS
FCOL = FF // RANKS
PROJ = 3 * QCOL + FCOL
PAIR = QCOL + FCOL
LOW = jnp.bfloat16
F32 = jnp.float32
BY_LAST = (((1,), (1,)), ((), ()))
BY_FIRST = (((0,), (0,)), ((), ()))


def adamw(weight, grad, first, second, decay):
    first = BETA_ONE * first + (1.0 - BETA_ONE) * grad
    second = BETA_TWO * second + (1.0 - BETA_TWO) * grad * grad
    first_hat = first / (1.0 - BETA_ONE**ADAM_STEP)
    second_hat = second / (1.0 - BETA_TWO**ADAM_STEP)
    weight = weight - LEARN_RATE * (first_hat / (jnp.sqrt(second_hat) + ADAM_EPS) + decay * weight)
    return (weight, first, second)


def dot(a, b, dims=(((1,), (0,)), ((), ()))):
    return lax.dot_general(a, b, dims, preferred_element_type=F32)


def turn(x, cosine, sin_low, sin_high):
    half = ROT // 2
    return x * cosine - pltpu.roll(x, QCOL - half, 1) * sin_low + pltpu.roll(x, half, 1) * sin_high


def block_middle(proj, gh, bias, cosine, sine, segc, segr, ah_ref, gp_ref, sum_ref, rows):
    length = proj.shape[0]
    half = ROT // 2
    lane = lax.broadcasted_iota(jnp.int32, (length, QCOL), 1)
    inner = lane % HEAD
    sin_low = jnp.where(inner < half, sine, 0.0)
    sin_high = jnp.where(inner >= half, sine, 0.0)
    q = turn(proj[:, :QCOL] + bias[:, :QCOL], cosine, sin_low, sin_high).astype(LOW)
    k = turn(
        proj[:, QCOL : 2 * QCOL] + bias[:, QCOL : 2 * QCOL], cosine, sin_low, sin_high
    ).astype(LOW)
    v = (proj[:, 2 * QCOL : 3 * QCOL] + bias[:, 2 * QCOL : 3 * QCOL]).astype(LOW)
    ga = gh[:, :QCOL].astype(LOW)
    row = lax.broadcasted_iota(jnp.int32, (length, length), 0)
    col = lax.broadcasted_iota(jnp.int32, (length, length), 1)
    allowed = (segc == segr) & (col <= row)
    zero = jnp.zeros((length, QCOL), LOW)
    attended = jnp.zeros((length, QCOL), F32)
    dq = jnp.zeros((length, QCOL), F32)
    dk = jnp.zeros((length, QCOL), F32)
    dv = jnp.zeros((length, QCOL), F32)
    for head in range(QCOL // HEAD):
        mine = (lane >= head * HEAD) & (lane < (head + 1) * HEAD)
        qh = jnp.where(mine, q, zero)
        kh = jnp.where(mine, k, zero)
        vh = jnp.where(mine, v, zero)
        gah = jnp.where(mine, ga, zero)
        scores = jnp.where(allowed, dot(qh, k, BY_LAST) * SCORE_SCALE, -1e30)
        peak = jnp.max(scores, axis=1, keepdims=True)
        grown = jnp.exp(scores - peak)
        probs = grown / jnp.sum(grown, axis=1, keepdims=True)
        low = probs.astype(LOW)
        attended = attended + dot(low, vh)
        dp = dot(gah, v, BY_LAST)
        dv = dv + dot(low, gah, BY_FIRST)
        ds = (probs * (dp - jnp.sum(probs * dp, axis=1, keepdims=True))).astype(LOW)
        dq = dq + dot(ds, kh)
        dk = dk + dot(ds, qh, BY_FIRST)
    ah_ref[rows, :QCOL] = attended.astype(LOW)
    dq = turn(dq * SCORE_SCALE, cosine, -sin_low, -sin_high).astype(LOW)
    dk = turn(dk * SCORE_SCALE, cosine, -sin_low, -sin_high).astype(LOW)
    dv = dv.astype(LOW)
    u = proj[:, 3 * QCOL :] + bias[:, 3 * QCOL :]
    c0 = 0.7978845608028654
    c1 = 0.044715
    square = u * u
    bent = jnp.tanh(c0 * (u + c1 * square * u))
    lift = 0.5 * (1.0 + bent)
    ah_ref[rows, QCOL:] = (u * lift).astype(LOW)
    slope = lift + 0.5 * u * (1.0 - bent * bent) * (c0 * (1.0 + 3.0 * c1 * square))
    df = (gh[:, QCOL:] * slope).astype(LOW)
    for at, part in ((0, dq), (QCOL, dk), (2 * QCOL, dv), (3 * QCOL, df)):
        width = part.shape[1]
        gp_ref[rows, at : at + width] = part
        sum_ref[:, at : at + width] += jnp.sum(part.astype(F32), axis=0, keepdims=True)


def chunk_kernel(
    n_own, n_y, n_c, n_cy, g_own, g_y, g_c, g_cy, w_cols, w_pair, bias, tail, cosine, sine, segc, segr,
    n_cat, g_cat, ah_out, gp_out, far_out, near_out, sums,
    n_s, g_s, gh_s, proj_s, ah_s, gp_s, far_s, near_s, in_sem, out_sem,
):
    length = n_own.shape[0]
    rows = 4 * length
    near = rows // 2
    wide = 256

    def into(pieces, held, sem):
        copies = [
            pltpu.make_async_copy(ref, held.at[pl.ds(i * length, length)], sem.at[i])
            for i, ref in enumerate(pieces)
        ]
        for one in copies:
            one.start()
        return copies

    g_in = into((g_own, g_y, g_c, g_cy), g_s, in_sem.at[0])
    n_in = into((n_own, n_y, n_c, n_cy), n_s, in_sem.at[1])
    for one in g_in:
        one.wait()
    drains = [pltpu.make_async_copy(g_s, g_cat, out_sem.at[0])]
    drains[-1].start()
    for at in range(0, PAIR, wide):
        upto = min(at + wide, PAIR)
        gh_s[:, at:upto] = dot(g_s[...], w_pair[at:upto, :], BY_LAST)
    for one in n_in:
        one.wait()
    drains.append(pltpu.make_async_copy(n_s, n_cat, out_sem.at[1]))
    drains[-1].start()
    for at in range(0, PROJ, wide):
        upto = min(at + wide, PROJ)
        proj_s[:, at:upto] = dot(n_s[...], w_cols[:, at:upto])
    sums[...] = jnp.zeros_like(sums)

    @pl.loop(0, 4)
    def _(i):
        at = pl.ds(pl.multiple_of(i * length, length), length)
        block_middle(
            proj_s[at, :],
            gh_s[at, :],
            bias[...],
            cosine[at, :],
            sine[at, :],
            segc[at, :],
            segr[i],
            ah_s,
            gp_s,
            sums,
            at,
        )

    for held, out in ((ah_s, ah_out), (gp_s, gp_out)):
        drains.append(pltpu.make_async_copy(held, out, out_sem.at[len(drains)]))
        drains[-1].start()

    @pl.loop(0, D // wide)
    def _(j):
        at = pl.ds(pl.multiple_of(j * wide, wide), wide)
        part = dot(gp_s[...], w_cols[at, :], BY_LAST)
        far_s[0, :, at] = part[near:].astype(LOW)
        near_s[0, :, at] = part[:near]

    for held, out in ((far_s, far_out), (near_s, near_out)):
        drains.append(pltpu.make_async_copy(held.at[0], out.at[0], out_sem.at[len(drains)]))
        drains[-1].start()

    @pl.loop(0, D // wide)
    def _(j):
        at = pl.ds(pl.multiple_of(j * wide, wide), wide)
        part = dot(ah_s[...], w_pair[:, at]) + tail[:, at]
        far_s[1, :, at] = part[near:].astype(LOW)
        near_s[1, :, at] = part[:near]

    for held, out in ((far_s, far_out), (near_s, near_out)):
        drains.append(pltpu.make_async_copy(held.at[1], out.at[1], out_sem.at[len(drains)]))
        drains[-1].start()
    for one in drains:
        one.wait()


def run_chunk(n_parts, g_parts, w_cols, w_pair, bias, tail, cosine, sine, segc, segr):
    length = n_parts[0].shape[0]
    rows = 4 * length
    near = rows // 2
    anywhere = pl.BlockSpec(memory_space=pl.ANY)
    here = pl.BlockSpec(memory_space=pltpu.VMEM)

    def shape(r, w, kind):
        return jax.ShapeDtypeStruct((r, w), kind)

    return pl.pallas_call(
        chunk_kernel,
        in_specs=[anywhere] * 8 + [here] * 8,
        out_specs=[anywhere] * 6 + [here],
        out_shape=[
            shape(rows, D, LOW),
            shape(rows, D, LOW),
            shape(rows, PAIR, LOW),
            shape(rows, PROJ, LOW),
            jax.ShapeDtypeStruct((2, near, D), LOW),
            jax.ShapeDtypeStruct((2, near, D), F32),
            shape(1, PROJ, F32),
        ],
        scratch_shapes=[
            pltpu.VMEM((rows, D), LOW),
            pltpu.VMEM((rows, D), LOW),
            pltpu.VMEM((rows, PAIR), F32),
            pltpu.VMEM((rows, PROJ), F32),
            pltpu.VMEM((rows, PAIR), LOW),
            pltpu.VMEM((rows, PROJ), LOW),
            pltpu.VMEM((2, near, D), LOW),
            pltpu.VMEM((2, near, D), F32),
            pltpu.SemaphoreType.DMA((2, 4)),
            pltpu.SemaphoreType.DMA((8,)),
        ],
        compiler_params=pltpu.CompilerParams(vmem_limit_bytes=44 * 2**20),
        cost_estimate=pl.CostEstimate(
            flops=4 * rows * D * (PROJ + PAIR) + 100 * rows * PROJ,
            bytes_accessed=rows * D * 16 + 4 * D * (PROJ + PAIR),
            transcendentals=rows * (2 * length + FCOL),
        ),
        name="chunk",
    )(*n_parts, *g_parts, w_cols, w_pair, bias, tail, cosine, sine, segc, segr)


def ranks_first(w_in, place, part):
    step = 16
    half = RANKS // 2

    def kernel(place_ref, w_ref, *outs):
        def put(rank, ref, at):
            for m in range(3):
                ref[at, :, m * QCOL : (m + 1) * QCOL] = w_ref[
                    :, m * D + rank * QCOL : m * D + (rank + 1) * QCOL
                ].astype(LOW)
            ref[at, :, 3 * QCOL :] = w_ref[
                :, 3 * D + rank * FCOL : 3 * D + (rank + 1) * FCOL
            ].astype(LOW)

        for rank in range(RANKS):
            put(rank, outs[-1], place_ref[rank])

        for n in range(NZ):
            outs[n][...] = outs[-1][2 * n : 2 * n + 2]
        outs[NZ][...] = outs[-1][half:]

    def block(count):
        return pl.BlockSpec((count, step, PROJ), lambda i, at: (0, i, 0))

    return pl.pallas_call(
        kernel,
        grid_spec=pltpu.PrefetchScalarGridSpec(
            num_scalar_prefetch=1,
            grid=(part // step,),
            in_specs=[
                pl.BlockSpec(
                    (step, 3 * D + FF), lambda i, at: (at[RANKS] * (part // step) + i, 0)
                )
            ],
            out_specs=[block(2)] * NZ + [block(half)],
            scratch_shapes=[pltpu.VMEM((RANKS, step, PROJ), LOW)],
        ),
        out_shape=[jax.ShapeDtypeStruct((2, part, PROJ), LOW)] * NZ
        + [jax.ShapeDtypeStruct((half, part, PROJ), LOW)],
        cost_estimate=pl.CostEstimate(
            flops=RANKS * part * PROJ, bytes_accessed=6 * RANKS * part * PROJ, transcendentals=0
        ),
        name="ranks_first",
    )(place, w_in)


def rows_home(pieces, place, part):
    each = pieces[0].shape[0]

    def kernel(place_ref, *refs):
        for i in range(2 * RANKS):
            at = pl.multiple_of(place_ref[i] * part, part)
            refs[-1][pl.ds(at, part), :] = refs[i // each][i % each]

    return pl.pallas_call(
        kernel,
        grid_spec=pltpu.PrefetchScalarGridSpec(
            num_scalar_prefetch=1,
            grid=(1,),
            in_specs=[pl.BlockSpec((each, part, PROJ), lambda i, at: (0, 0, 0))] * len(pieces),
            out_specs=pl.BlockSpec((D, PROJ), lambda i, at: (0, 0)),
        ),
        out_shape=jax.ShapeDtypeStruct((D, PROJ), LOW),
        cost_estimate=pl.CostEstimate(flops=0, bytes_accessed=4 * D * PROJ, transcendentals=0),
        name="rows_home",
    )(place, *pieces)


def split_sum(grads, held, place, part, first, blocks, kind):
    def kernel(place_ref, *refs):
        total = refs[0][...]
        for ref in refs[1 : len(grads)]:
            total = total + ref[...]
        copy = place_ref[RANKS]

        def give(sent, kept):
            refs[-2][...] = sent.astype(kind)
            for ref in refs[len(grads) : -2]:
                kept = kept + ref[...]
            refs[-1][...] = kept

        @pl.when(copy == 0)
        def _():
            give(total[:, 1], total[:, 0])

        @pl.when(copy != 0)
        def _():
            give(total[:, 0], total[:, 1])

    own = pl.BlockSpec((1, 2, part, PROJ), lambda i, at: (at[first + i], 0, 0, 0))
    old = pl.BlockSpec((1, part, PROJ), lambda i, at: (first + i, 0, 0))
    half = pl.BlockSpec((1, part, PROJ), lambda i, at: (i, 0, 0))
    return pl.pallas_call(
        kernel,
        grid_spec=pltpu.PrefetchScalarGridSpec(
            num_scalar_prefetch=1,
            grid=(blocks,),
            in_specs=[own] * len(grads) + [old] * len(held),
            out_specs=[half, half],
        ),
        out_shape=[
            jax.ShapeDtypeStruct((blocks, part, PROJ), kind),
            jax.ShapeDtypeStruct((blocks, part, PROJ), F32),
        ],
        cost_estimate=pl.CostEstimate(
            flops=8 * blocks * part * PROJ,
            bytes_accessed=30 * blocks * part * PROJ,
            transcendentals=0,
        ),
        name="split_sum",
    )(place, *[g.reshape(RANKS, 2, part, PROJ) for g in grads], *held)


def adamw_rows(weight, first, second, grads, slots, before=None):
    rows, cols = weight.shape
    part = rows // 2
    wide = D
    steps = cols // wide

    def kernel(slots_ref, w_ref, m_ref, v_ref, grads_ref, *refs):
        g_out, w_out, m_out, v_out = refs[-5:-1]
        grad_s = refs[-1]
        j = pl.program_id(0)

        @pl.when(j < 3)
        def _():
            at = pl.ds(pl.multiple_of(j * QCOL, QCOL), QCOL)
            for rank in range(RANKS):
                grad_s[:, rank * QCOL : (rank + 1) * QCOL] = grads_ref[
                    slots_ref[rank], :, at
                ].astype(F32)

        @pl.when(j >= 3)
        def _():
            per = D // FCOL
            for m in range(per):
                grad_s[:, m * FCOL : (m + 1) * FCOL] = grads_ref[
                    slots_ref[per * (j - 3) + m], :, 3 * QCOL :
                ].astype(F32)

        grad = grad_s[...]
        new_w, new_m, new_v = adamw(w_ref[...], grad, m_ref[...], v_ref[...], DECAY)
        g_out[...] = grad
        w_out[...] = new_w
        m_out[...] = new_m
        v_out[...] = new_v

    slab = pl.BlockSpec((part, wide), lambda j, at: (at[RANKS], j))
    held = [] if before is None else list(before)
    return pl.pallas_call(
        kernel,
        grid_spec=pltpu.PrefetchScalarGridSpec(
            num_scalar_prefetch=1,
            grid=(steps,),
            in_specs=[slab] * 3
            + [pl.BlockSpec((RANKS, part, PROJ), lambda j, at: (0, 0, 0))]
            + [pl.BlockSpec(memory_space=pl.ANY)] * len(held),
            out_specs=[slab] * 4,
            scratch_shapes=[pltpu.VMEM((part, wide), F32)],
        ),
        out_shape=[jax.ShapeDtypeStruct((rows, cols), F32)] * 4,
        input_output_aliases={5 + i: i for i in range(len(held))},
        cost_estimate=pl.CostEstimate(
            flops=20 * part * cols, bytes_accessed=30 * part * cols, transcendentals=part * cols
        ),
        name="adamw_rows",
    )(slots, weight, first, second, grads, *held)


def make_on_device(mesh):
    shards = mesh.shape["shard"]
    copies = mesh.shape["replica"]
    fold = shards // RANKS
    rank_of = lambda z, y, c: (z * 2 + y) * 2 + c

    def moves(target):
        pairs = []
        for z in range(NZ):
            for y in range(2):
                for c in range(2):
                    to = rank_of(*target(z, y, c))
                    for f in range(fold):
                        pairs.append((rank_of(z, y, c) * fold + f, to * fold + f))
        return pairs

    swap_core = moves(lambda z, y, c: (z, y, 1 - c))
    swap_y = moves(lambda z, y, c: (z, 1 - y, c))
    up_z = [moves(lambda z, y, c, n=n: ((z + n) % NZ, y, c)) for n in range(NZ)]

    def core(x):
        return lax.ppermute(x, "shard", swap_core)

    def across_y(x):
        return lax.ppermute(x, "shard", swap_y)

    def along_z(x, n):
        return lax.ppermute(x, "shard", up_z[n % NZ])

    def across_fold(x, n):
        return lax.ppermute(
            x,
            "shard",
            [(r * fold + f, r * fold + (f + n) % fold) for r in range(RANKS) for f in range(fold)],
        )

    def next_copy(x, n):
        return lax.ppermute(x, "replica", [(i, (i + n) % copies) for i in range(copies)])

    def fold_gather(x, f):
        if fold == 1:
            return x
        parts = jnp.stack([x] + [across_fold(x, n) for n in range(1, fold)])
        order = (f - jnp.arange(fold)) % fold
        return jnp.take(parts, order, axis=0).reshape((fold * x.shape[0],) + x.shape[1:])

    def fold_scatter(x, f):
        if fold == 1:
            return x
        parts = x.reshape((fold, x.shape[0] // fold) + x.shape[1:])
        total = lax.dynamic_index_in_dim(parts, f, 0, keepdims=False)
        for n in range(1, fold):
            part = lax.dynamic_index_in_dim(parts, (f + n) % fold, 0, keepdims=False)
            total = total + across_fold(part, n).astype(F32)
        return total

    def gather_z(x):
        above = along_z(x, 3)
        below = along_z(x, 1)
        opposite = along_z(above, 3)
        chunks = []
        for x in (x, below, opposite, above):
            flipped = across_y(x)
            far = core(x)
            chunks.append((x, flipped, far, core(flipped)))
        return chunks

    def table(me, entries):
        rows = [
            entries(r // 4, r // 2 % 2, r % 2) for r in range(RANKS) for _ in range(fold)
        ]
        return lax.dynamic_index_in_dim(jnp.array(rows, dtype=jnp.int32), me, 0, keepdims=False)

    def near(z, y, c, n, dy, dc):
        return rank_of((z + n) % NZ, (y + dy) % 2, (c + dc) % 2)

    def columns_of(w_in, me, z, y, c, f, copy):
        rows = w_in.shape[0] * fold
        part = rows // copies
        if fold == 1 and copies == 2:
            def slots(z, y, c):
                order = [near(z, y, c, n, i, j) for j in (0, 1) for n in range(NZ) for i in (0, 1)]
                return [order.index(r) for r in range(RANKS)]

            place = jnp.concatenate([table(me, slots), copy.reshape(1)])
            *kept, sent = ranks_first(w_in, place, part)
            came = core(sent).reshape(NZ, 2, part, PROJ)
            pieces = []
            for n in (0, 2, 1, 3):
                piece = jnp.stack([kept[n], came[n]], axis=1)
                if n:
                    piece = along_z(piece, n)
                over = across_y(piece[1])
                piece = jnp.concatenate([piece[0], over])
                pieces.append((piece, next_copy(piece, 1)))
            home = table(
                me,
                lambda z, y, c: [
                    2 * near(z, y, c, -n, i, j) for n in (0, 2, 1, 3) for i in (0, 1) for j in (0, 1)
                ],
            )
            home = jnp.concatenate([home + copy, home + (1 - copy)])
            return rows_home([p[0] for p in pieces] + [p[1] for p in pieces], home, part)
        low_in = fold_gather(w_in.astype(LOW), f)
        by_rank = jnp.concatenate(
            [
                low_in[:, :D].reshape(rows, RANKS, QCOL),
                low_in[:, D : 2 * D].reshape(rows, RANKS, QCOL),
                low_in[:, 2 * D : 3 * D].reshape(rows, RANKS, QCOL),
                low_in[:, 3 * D :].reshape(rows, RANKS, FCOL),
            ],
            axis=2,
        )
        turned = by_rank.transpose(1, 0, 2).reshape(NZ, 2, 2, rows, PROJ)
        return to_ranks(turned, z, y, c).reshape(D, PROJ)

    def to_ranks(blocks, z, y, c):
        kept = lax.dynamic_index_in_dim(blocks, c, 2, keepdims=False)
        came = core(lax.dynamic_index_in_dim(blocks, 1 - c, 2, keepdims=False))
        blocks = jnp.stack([jnp.where(c == 0, kept, came), jnp.where(c == 0, came, kept)], axis=2)
        kept = lax.dynamic_index_in_dim(blocks, y, 1, keepdims=False)
        came = across_y(lax.dynamic_index_in_dim(blocks, 1 - y, 1, keepdims=False))
        blocks = jnp.stack([jnp.where(y == 0, kept, came), jnp.where(y == 0, came, kept)], axis=1)
        by_z = [lax.dynamic_index_in_dim(blocks, z, 0, keepdims=False)]
        for n in range(1, NZ):
            by_z.append(
                along_z(lax.dynamic_index_in_dim(blocks, (z + n) % NZ, 0, keepdims=False), n)
            )
        return jnp.take(jnp.stack(by_z), (z - jnp.arange(NZ)) % NZ, axis=0)

    def start_in(grad_in, me, copy):
        part = D // RANKS // 2
        place = table(
            me,
            lambda z, y, c: [near(z, y, c, n, i, j) for n in GRAD_ORDER for i in (0, 1) for j in (0, 1)],
        )
        place = jnp.concatenate([place, copy.reshape(1)])
        sent, kept = split_sum(grad_in, (), place, part, 0, RANKS, F32)
        return place, kept, next_copy(sent, 1)

    def finish_in(grad_in, early, w_in, m_in, v_in, me, z, y, c, f, copy):
        rows = w_in.shape[0] * fold
        part = rows // copies
        if fold == 1 and copies == 2:
            place, kept, heard = early
            halves = []
            for i, n in enumerate(GRAD_ORDER):
                sent, base = split_sum(
                    grad_in[EARLY:], (kept, heard), place, part, 4 * i, 4, LOW
                )
                late = next_copy(sent, 1)
                block = (base + late).astype(LOW)
                if n:
                    block = along_z(block, n)
                came = across_y(block[2:])
                block = jnp.stack([block[:2], came])
                came = core(block[:, 1])
                block = jnp.stack([block[:, 0], came], axis=1)
                block = block.reshape(4, part, PROJ)
                came = next_copy(block, 1)
                halves.append((block, came))
            own = jnp.concatenate([h[0] for h in halves])
            other = jnp.concatenate([h[1] for h in halves])

            def slots(z, y, c):
                order = [near(z, y, c, -n, i, j) for n in GRAD_ORDER for i in (0, 1) for j in (0, 1)]
                return [order.index(r) for r in range(RANKS)]

            slot = table(me, slots)
            mine = jnp.concatenate([slot, copy.reshape(1)])
            theirs = jnp.concatenate([slot, 1 - copy.reshape(1)])
            first = adamw_rows(w_in, m_in, v_in, own, mine)
            return adamw_rows(w_in, m_in, v_in, other, theirs, first)
        grad_in = sum(grad_in[1:], grad_in[0])
        back = to_ranks(grad_in.astype(LOW).reshape(NZ, 2, 2, rows, PROJ), z, y, c)
        both = back.reshape(RANKS, rows, PROJ).transpose(1, 0, 2)
        both = jnp.concatenate(
            [
                both[:, :, :QCOL].reshape(rows, D),
                both[:, :, QCOL : 2 * QCOL].reshape(rows, D),
                both[:, :, 2 * QCOL : 3 * QCOL].reshape(rows, D),
                both[:, :, 3 * QCOL :].reshape(rows, FF),
            ],
            axis=1,
        )
        grad = fold_scatter(both, f).astype(F32)
        for moved in [next_copy(grad, n) for n in range(1, copies)]:
            grad = grad + moved
        return (grad,) + adamw(w_in, grad, m_in, v_in, DECAY)

    def on_device(
        tokens,
        seg_ids,
        cotangent,
        w_in,
        w_out,
        w_fc2,
        vectors,
        m_in,
        v_in,
        m_out,
        v_out,
        m_fc2,
        v_fc2,
        m_vec,
        v_vec,
    ):
        length = tokens.shape[0]
        me = lax.axis_index("shard")
        copy = lax.axis_index("replica")
        t = me // fold
        f = me % fold
        z, y, c = t // 4, (t // 2) % 2, t % 2

        g_chunks = gather_z(cotangent)

        w_cols = columns_of(w_in, me, z, y, c, f, copy)
        w_pair = jnp.concatenate(
            [fold_gather(w_out.astype(LOW), f), fold_gather(w_fc2.astype(LOW), f)], axis=0
        )

        order = jnp.arange(length, dtype=jnp.int32)
        same = seg_ids[:, None] == seg_ids[None, :]
        place = jnp.sum((same & (order[None, :] < order[:, None])).astype(F32), axis=1)
        grouped = fold_gather(vectors.reshape(-1, 11), f)
        small = jnp.concatenate([grouped[:, 9], grouped[:, 10], seg_ids.astype(F32), place])
        small = small.reshape(1, -1)
        heard = [small]
        for n in range(1, NZ):
            heard.append(along_z(small, n))
        small = jnp.concatenate(heard, axis=0)
        small = jnp.stack([small, across_y(small)], axis=1)
        small = jnp.stack([small, core(small)], axis=2)
        gains = small[..., : 2 * QCOL]
        gains = jnp.take(gains, (z - jnp.arange(NZ)) % NZ, axis=0)
        gains = jnp.where(y == 0, gains, gains[:, ::-1])
        gains = jnp.where(c == 0, gains, gains[:, :, ::-1]).reshape(RANKS, 2, QCOL)
        gain = gains[:, 0].reshape(D)
        shift = gains[:, 1].reshape(D)
        tail = small[..., 2 * QCOL :].transpose(0, 2, 1, 3).reshape(NZ, 4, 2, length)
        segs = tail[:, :, 0]
        places = tail[:, :, 1]
        lane = jnp.arange(QCOL, dtype=jnp.int32) % HEAD
        freqs = 10000.0 ** (-(lane % (ROT // 2)).astype(F32) * (2.0 / ROT))
        freqs = jnp.where(lane < ROT, freqs, 0.0)
        inputs = tokens.astype(F32)
        centred = inputs - jnp.mean(inputs, axis=1, keepdims=True)
        inv_std = lax.rsqrt(jnp.mean(centred * centred, axis=1, keepdims=True) + NORM_EPS)
        standard = centred * inv_std
        normed = (standard * gain + shift).astype(LOW)
        n_chunks = gather_z(normed)

        bias_in = jnp.concatenate(
            [grouped[:, 0], grouped[:, 1], grouped[:, 2], grouped[:, 3:7].reshape(FCOL)]
        ).reshape(1, PROJ)
        bias_tail = lax.dynamic_update_slice(
            jnp.zeros((D,), F32), grouped[:, 7] + grouped[:, 8], (t * QCOL,)
        )

        def scatter_add(near, far, n, carried):
            came = core(far)
            sent = (near[:, length:] + came[:, length:].astype(F32)).astype(LOW)
            over = across_y(sent)
            own = near[:, :length] + came[:, :length].astype(F32) + over.astype(F32)
            if carried is not None:
                own = own + carried
            if n == 0:
                return own
            return along_z(own.astype(LOW), 1 if n == 3 else 3).astype(F32)

        totals = []
        early = None
        grad_in = []
        grad_pair = []
        proj_sum = []
        for n in CHUNKS:
            gc = g_chunks[n]
            nc = n_chunks[n]
            if grad_in:
                gc, nc, last_in, last_pair = lax.optimization_barrier(
                    (gc, nc, grad_in[-1], grad_pair[-1])
                )
                grad_in[-1] = last_in
                grad_pair[-1] = last_pair
            angles = places[n].reshape(4 * length, 1) * freqs
            n_cat, g_cat, ah, gp, far, near, sums = run_chunk(
                nc,
                gc,
                w_cols,
                w_pair,
                bias_in,
                bias_tail.reshape(1, D),
                jnp.cos(angles),
                jnp.sin(angles),
                segs[n].reshape(4 * length, 1),
                segs[n].reshape(4, 1, length),
            )
            grad_in.append(dot(n_cat, gp, BY_FIRST))
            grad_pair.append(dot(ah, g_cat, BY_FIRST))
            proj_sum.append(sums)
            carried = scatter_add(near, far, n, totals.pop() if n == 1 else None)
            totals.append(carried)
            if len(grad_in) == EARLY and fold == 1 and copies == 2:
                early = start_in(grad_in, me, copy)
        gn_total = sum([part[0] for part in totals[1:]], totals[0][0])
        out_total = sum([part[1] for part in totals[1:]], totals[0][1])
        proj_sum = sum(proj_sum[1:], proj_sum[0])
        grad_pair = sum(grad_pair[1:], grad_pair[0])

        output = (inputs + out_total).astype(LOW)
        upstream = cotangent.astype(F32)
        scaled = gn_total * gain
        grad_tokens = upstream + inv_std * (
            scaled
            - jnp.mean(scaled, axis=1, keepdims=True)
            - standard * jnp.mean(scaled * standard, axis=1, keepdims=True)
        )

        sums = jnp.stack(
            [jnp.sum(upstream, axis=0), jnp.sum(gn_total * standard, axis=0), jnp.sum(gn_total, axis=0)]
        )
        sums = sums + core(sums)
        sums = sums + across_y(sums)
        for moved in [along_z(sums, n) for n in range(1, NZ)]:
            sums = sums + moved
        sums = lax.dynamic_slice(sums, (0, t * QCOL), (3, QCOL))
        vec = jnp.concatenate(
            [
                proj_sum[0, : 3 * QCOL].reshape(3, QCOL).T,
                proj_sum[0, 3 * QCOL :].reshape(QCOL, 4),
                sums[0][:, None],
                sums[0][:, None],
                sums[1][:, None],
                sums[2][:, None],
            ],
            axis=1,
        )
        vec = fold_scatter(vec, f).reshape(-1)
        for moved in [next_copy(vec, n) for n in range(1, copies)]:
            vec = vec + moved

        g_out = fold_scatter(grad_pair[:QCOL], f)
        g_fc2 = fold_scatter(grad_pair[QCOL:], f)
        g_pair = jnp.concatenate([g_out, g_fc2], axis=0).astype(LOW)
        pair_total = g_pair.astype(F32)
        for n in range(1, copies):
            pair_total = pair_total + next_copy(g_pair, n).astype(F32)
        grad_out = pair_total[: g_out.shape[0]]
        grad_fc2 = pair_total[g_out.shape[0] :]

        grad_w_in, new_in, new_m_in, new_v_in = finish_in(
            grad_in, early, w_in, m_in, v_in, me, z, y, c, f, copy
        )
        new_out, new_m_out, new_v_out = adamw(w_out, grad_out, m_out, v_out, DECAY)
        new_fc2, new_m_fc2, new_v_fc2 = adamw(w_fc2, grad_fc2, m_fc2, v_fc2, DECAY)
        new_vec, new_m_vec, new_v_vec = adamw(vectors, vec, m_vec, v_vec, 0.0)
        return (
            output,
            grad_tokens,
            grad_w_in,
            grad_out,
            grad_fc2,
            vec,
            new_in,
            new_out,
            new_fc2,
            new_vec,
            new_m_in,
            new_v_in,
            new_m_out,
            new_v_out,
            new_m_fc2,
            new_v_fc2,
            new_m_vec,
            new_v_vec,
        )

    return on_device


def solution(mesh):
    both = P(("replica", "shard"), None)
    flat = P("shard")
    rows = P("shard", None)
    return jax.shard_map(
        make_on_device(mesh),
        mesh=mesh,
        in_specs=(both, P(("replica", "shard")), both, rows, rows, rows, flat)
        + (rows,) * 6
        + (flat, flat),
        out_specs=(both, both, rows, rows, rows, flat)
        + (rows, rows, rows, flat)
        + (rows,) * 6
        + (flat, flat),
        check_vma=False,
    )
```

```python
import jax
import jax.numpy as jnp
from jax import lax
from jax.experimental import pallas as pl
from jax.experimental.pallas import tpu as pltpu
from jax.sharding import PartitionSpec as P


D = 2048
FF = 8192
HEAD = 64
ROT = 32
ADAM_STEP = 4

NORM_EPS = 1e-05
SCORE_SCALE = 0.125
LEARN_RATE = 0.02
BETA_ONE = 0.9
BETA_TWO = 0.98
ADAM_EPS = 1e-08
DECAY = 0.1

RANKS = 16
NZ = 4
CHUNKS = (0, 3, 2, 1)
GRAD_ORDER = (2, 3, 1, 0)
EARLY = 2
QCOL = D // RANKS
FCOL = FF // RANKS
PROJ = 3 * QCOL + FCOL
PAIR = QCOL + FCOL
LOW = jnp.bfloat16
F32 = jnp.float32
BY_LAST = (((1,), (1,)), ((), ()))
BY_FIRST = (((0,), (0,)), ((), ()))


def adamw(weight, grad, first, second, decay):
    first = BETA_ONE * first + (1.0 - BETA_ONE) * grad
    second = BETA_TWO * second + (1.0 - BETA_TWO) * grad * grad
    first_hat = first * (1.0 / (1.0 - BETA_ONE**ADAM_STEP))
    second_hat = second * (1.0 / (1.0 - BETA_TWO**ADAM_STEP))
    weight = weight - LEARN_RATE * (first_hat / (jnp.sqrt(second_hat) + ADAM_EPS) + decay * weight)
    return (weight, first, second)


def dot(a, b, dims=(((1,), (0,)), ((), ()))):
    return lax.dot_general(a, b, dims, preferred_element_type=F32)


def turn(x, cosine, sin_low, sin_high):
    half = ROT // 2
    return x * cosine - pltpu.roll(x, QCOL - half, 1) * sin_low + pltpu.roll(x, half, 1) * sin_high


def block_middle(proj, gh, bias, cosine, sine, segc, segr, ah_ref, gp_ref, sum_ref, rows):
    length = proj.shape[0]
    half = ROT // 2
    lane = lax.broadcasted_iota(jnp.int32, (length, QCOL), 1)
    inner = lane % HEAD
    sin_low = jnp.where(inner < half, sine, 0.0)
    sin_high = jnp.where(inner >= half, sine, 0.0)
    q = turn(proj[:, :QCOL] + bias[:, :QCOL], cosine, sin_low, sin_high).astype(LOW)
    k = turn(
        proj[:, QCOL : 2 * QCOL] + bias[:, QCOL : 2 * QCOL], cosine, sin_low, sin_high
    ).astype(LOW)
    v = (proj[:, 2 * QCOL : 3 * QCOL] + bias[:, 2 * QCOL : 3 * QCOL]).astype(LOW)
    ga = gh[:, :QCOL].astype(LOW)
    row = lax.broadcasted_iota(jnp.int32, (length, length), 0)
    col = lax.broadcasted_iota(jnp.int32, (length, length), 1)
    allowed = (segc == segr) & (col <= row)
    zero = jnp.zeros((length, QCOL), LOW)
    attended = jnp.zeros((length, QCOL), F32)
    dq = jnp.zeros((length, QCOL), F32)
    dk = jnp.zeros((length, QCOL), F32)
    dv = jnp.zeros((length, QCOL), F32)
    for head in range(QCOL // HEAD):
        mine = (lane >= head * HEAD) & (lane < (head + 1) * HEAD)
        qh = jnp.where(mine, q, zero)
        kh = jnp.where(mine, k, zero)
        vh = jnp.where(mine, v, zero)
        gah = jnp.where(mine, ga, zero)
        scores = jnp.where(allowed, dot(qh, k, BY_LAST) * SCORE_SCALE, -1e30)
        peak = jnp.max(scores, axis=1, keepdims=True)
        grown = jnp.exp(scores - peak)
        probs = grown * (1.0 / jnp.sum(grown, axis=1, keepdims=True))
        low = probs.astype(LOW)
        attended = attended + dot(low, vh)
        dp = dot(gah, v, BY_LAST)
        dv = dv + dot(low, gah, BY_FIRST)
        ds = (probs * (dp - jnp.sum(probs * dp, axis=1, keepdims=True))).astype(LOW)
        dq = dq + dot(ds, kh)
        dk = dk + dot(ds, qh, BY_FIRST)
    ah_ref[rows, :QCOL] = attended.astype(LOW)
    dq = turn(dq * SCORE_SCALE, cosine, -sin_low, -sin_high).astype(LOW)
    dk = turn(dk * SCORE_SCALE, cosine, -sin_low, -sin_high).astype(LOW)
    dv = dv.astype(LOW)
    u = proj[:, 3 * QCOL :] + bias[:, 3 * QCOL :]
    c0 = 0.7978845608028654
    c1 = 0.044715
    square = u * u
    bent = jnp.tanh(c0 * (u + c1 * square * u))
    lift = 0.5 * (1.0 + bent)
    ah_ref[rows, QCOL:] = (u * lift).astype(LOW)
    slope = lift + 0.5 * u * (1.0 - bent * bent) * (c0 * (1.0 + 3.0 * c1 * square))
    df = (gh[:, QCOL:] * slope).astype(LOW)
    for at, part in ((0, dq), (QCOL, dk), (2 * QCOL, dv), (3 * QCOL, df)):
        width = part.shape[1]
        gp_ref[rows, at : at + width] = part
        sum_ref[:, at : at + width] += jnp.sum(part.astype(F32), axis=0, keepdims=True)


def chunk_kernel(
    n_own, n_y, n_c, n_cy, g_own, g_y, g_c, g_cy, w_cols, w_pair, bias, tail, cosine, sine, segc, segr,
    n_cat, g_cat, ah_out, gp_out, far_out, near_out, sums,
    n_s, g_s, gh_s, proj_s, ah_s, gp_s, far_s, near_s, in_sem, out_sem,
):
    length = n_own.shape[0]
    rows = 4 * length
    near = rows // 2
    wide = 256

    def into(pieces, held, sem):
        copies = [
            pltpu.make_async_copy(ref, held.at[pl.ds(i * length, length)], sem.at[i])
            for i, ref in enumerate(pieces)
        ]
        for one in copies:
            one.start()
        return copies

    g_in = into((g_own, g_y, g_c, g_cy), g_s, in_sem.at[0])
    n_in = into((n_own, n_y, n_c, n_cy), n_s, in_sem.at[1])
    for one in g_in:
        one.wait()
    drains = [pltpu.make_async_copy(g_s, g_cat, out_sem.at[0])]
    drains[-1].start()
    for at in range(0, PAIR, wide):
        upto = min(at + wide, PAIR)
        gh_s[:, at:upto] = dot(g_s[...], w_pair[at:upto, :], BY_LAST)
    for one in n_in:
        one.wait()
    drains.append(pltpu.make_async_copy(n_s, n_cat, out_sem.at[1]))
    drains[-1].start()
    for at in range(0, PROJ, wide):
        upto = min(at + wide, PROJ)
        proj_s[:, at:upto] = dot(n_s[...], w_cols[:, at:upto])
    sums[...] = jnp.zeros_like(sums)

    @pl.loop(0, 4)
    def _(i):
        at = pl.ds(pl.multiple_of(i * length, length), length)
        block_middle(
            proj_s[at, :],
            gh_s[at, :],
            bias[...],
            cosine[at, :],
            sine[at, :],
            segc[at, :],
            segr[i],
            ah_s,
            gp_s,
            sums,
            at,
        )

    for held, out in ((ah_s, ah_out), (gp_s, gp_out)):
        drains.append(pltpu.make_async_copy(held, out, out_sem.at[len(drains)]))
        drains[-1].start()

    @pl.loop(0, D // wide)
    def _(j):
        at = pl.ds(pl.multiple_of(j * wide, wide), wide)
        part = dot(gp_s[...], w_cols[at, :], BY_LAST)
        far_s[0, :, at] = part[near:].astype(LOW)
        near_s[0, :, at] = part[:near]

    for held, out in ((far_s, far_out), (near_s, near_out)):
        drains.append(pltpu.make_async_copy(held.at[0], out.at[0], out_sem.at[len(drains)]))
        drains[-1].start()

    @pl.loop(0, D // wide)
    def _(j):
        at = pl.ds(pl.multiple_of(j * wide, wide), wide)
        part = dot(ah_s[...], w_pair[:, at]) + tail[:, at]
        far_s[1, :, at] = part[near:].astype(LOW)
        near_s[1, :, at] = part[:near]

    for held, out in ((far_s, far_out), (near_s, near_out)):
        drains.append(pltpu.make_async_copy(held.at[1], out.at[1], out_sem.at[len(drains)]))
        drains[-1].start()
    for one in drains:
        one.wait()


def run_chunk(n_parts, g_parts, w_cols, w_pair, bias, tail, cosine, sine, segc, segr):
    length = n_parts[0].shape[0]
    rows = 4 * length
    near = rows // 2
    anywhere = pl.BlockSpec(memory_space=pl.ANY)
    here = pl.BlockSpec(memory_space=pltpu.VMEM)

    def shape(r, w, kind):
        return jax.ShapeDtypeStruct((r, w), kind)

    return pl.pallas_call(
        chunk_kernel,
        in_specs=[anywhere] * 8 + [here] * 8,
        out_specs=[anywhere] * 6 + [here],
        out_shape=[
            shape(rows, D, LOW),
            shape(rows, D, LOW),
            shape(rows, PAIR, LOW),
            shape(rows, PROJ, LOW),
            jax.ShapeDtypeStruct((2, near, D), LOW),
            jax.ShapeDtypeStruct((2, near, D), F32),
            shape(1, PROJ, F32),
        ],
        scratch_shapes=[
            pltpu.VMEM((rows, D), LOW),
            pltpu.VMEM((rows, D), LOW),
            pltpu.VMEM((rows, PAIR), F32),
            pltpu.VMEM((rows, PROJ), F32),
            pltpu.VMEM((rows, PAIR), LOW),
            pltpu.VMEM((rows, PROJ), LOW),
            pltpu.VMEM((2, near, D), LOW),
            pltpu.VMEM((2, near, D), F32),
            pltpu.SemaphoreType.DMA((2, 4)),
            pltpu.SemaphoreType.DMA((8,)),
        ],
        compiler_params=pltpu.CompilerParams(vmem_limit_bytes=44 * 2**20),
        cost_estimate=pl.CostEstimate(
            flops=4 * rows * D * (PROJ + PAIR) + 100 * rows * PROJ,
            bytes_accessed=rows * D * 16 + 4 * D * (PROJ + PAIR),
            transcendentals=rows * (2 * length + FCOL),
        ),
        name="chunk",
    )(*n_parts, *g_parts, w_cols, w_pair, bias, tail, cosine, sine, segc, segr)


def ranks_first(w_in, place, part):
    step = 16
    half = RANKS // 2

    def kernel(place_ref, w_ref, *outs):
        def put(rank, ref, at):
            for m in range(3):
                ref[at, :, m * QCOL : (m + 1) * QCOL] = w_ref[
                    :, m * D + rank * QCOL : m * D + (rank + 1) * QCOL
                ].astype(LOW)
            ref[at, :, 3 * QCOL :] = w_ref[
                :, 3 * D + rank * FCOL : 3 * D + (rank + 1) * FCOL
            ].astype(LOW)

        for rank in range(RANKS):
            put(rank, outs[-1], place_ref[rank])

        for n in range(NZ):
            outs[n][...] = outs[-1][2 * n : 2 * n + 2]
        outs[NZ][...] = outs[-1][half:]

    def block(count):
        return pl.BlockSpec((count, step, PROJ), lambda i, at: (0, i, 0))

    return pl.pallas_call(
        kernel,
        grid_spec=pltpu.PrefetchScalarGridSpec(
            num_scalar_prefetch=1,
            grid=(part // step,),
            in_specs=[
                pl.BlockSpec(
                    (step, 3 * D + FF), lambda i, at: (at[RANKS] * (part // step) + i, 0)
                )
            ],
            out_specs=[block(2)] * NZ + [block(half)],
            scratch_shapes=[pltpu.VMEM((RANKS, step, PROJ), LOW)],
        ),
        out_shape=[jax.ShapeDtypeStruct((2, part, PROJ), LOW)] * NZ
        + [jax.ShapeDtypeStruct((half, part, PROJ), LOW)],
        cost_estimate=pl.CostEstimate(
            flops=RANKS * part * PROJ, bytes_accessed=6 * RANKS * part * PROJ, transcendentals=0
        ),
        name="ranks_first",
    )(place, w_in)


def rows_home(pieces, place, part):
    each = pieces[0].shape[0]

    def kernel(place_ref, *refs):
        for i in range(2 * RANKS):
            at = pl.multiple_of(place_ref[i] * part, part)
            refs[-1][pl.ds(at, part), :] = refs[i // each][i % each]

    return pl.pallas_call(
        kernel,
        grid_spec=pltpu.PrefetchScalarGridSpec(
            num_scalar_prefetch=1,
            grid=(1,),
            in_specs=[pl.BlockSpec((each, part, PROJ), lambda i, at: (0, 0, 0))] * len(pieces),
            out_specs=pl.BlockSpec((D, PROJ), lambda i, at: (0, 0)),
        ),
        out_shape=jax.ShapeDtypeStruct((D, PROJ), LOW),
        cost_estimate=pl.CostEstimate(flops=0, bytes_accessed=4 * D * PROJ, transcendentals=0),
        name="rows_home",
    )(place, *pieces)


def split_sum(grads, held, place, part, first, groups, kind):
    step = part // 2

    def kernel(place_ref, *refs):
        copy = place_ref[NZ + 4]
        for k in range(4):
            at = place_ref[NZ + k]

            def total(half):
                value = refs[0][at, half]
                for ref in refs[1 : len(grads)]:
                    value = value + ref[at, half]
                return value

            refs[-2][k] = total(1 - copy).astype(kind)
            kept = total(copy)
            for ref in refs[len(grads) : -2]:
                kept = kept + ref[k]
            refs[-1][k] = kept

    own = pl.BlockSpec((4, 2, step, PROJ), lambda i, j, at: (at[first + i], 0, j, 0))
    old = pl.BlockSpec((4, step, PROJ), lambda i, j, at: (first + i, j, 0))
    half = pl.BlockSpec((4, step, PROJ), lambda i, j, at: (i, j, 0))
    return pl.pallas_call(
        kernel,
        grid_spec=pltpu.PrefetchScalarGridSpec(
            num_scalar_prefetch=1,
            grid=(groups, 2),
            in_specs=[own] * len(grads) + [old] * len(held),
            out_specs=[half, half],
        ),
        out_shape=[
            jax.ShapeDtypeStruct((4 * groups, part, PROJ), kind),
            jax.ShapeDtypeStruct((4 * groups, part, PROJ), F32),
        ],
        cost_estimate=pl.CostEstimate(
            flops=32 * groups * part * PROJ,
            bytes_accessed=120 * groups * part * PROJ,
            transcendentals=0,
        ),
        name="split_sum",
    )(place, *[g.reshape(RANKS, 2, part, PROJ) for g in grads], *held)


def adamw_rows(weight, first, second, grads, slots, before=None):
    rows, cols = weight.shape
    part = rows // 2
    wide = D
    steps = cols // wide

    def kernel(slots_ref, w_ref, m_ref, v_ref, grads_ref, *refs):
        g_out, w_out, m_out, v_out = refs[-5:-1]
        grad_s = refs[-1]
        j = pl.program_id(0)

        @pl.when(j < 3)
        def _():
            at = pl.ds(pl.multiple_of(j * QCOL, QCOL), QCOL)
            for rank in range(RANKS):
                grad_s[:, rank * QCOL : (rank + 1) * QCOL] = grads_ref[
                    slots_ref[rank], :, at
                ].astype(F32)

        @pl.when(j >= 3)
        def _():
            per = D // FCOL
            for m in range(per):
                grad_s[:, m * FCOL : (m + 1) * FCOL] = grads_ref[
                    slots_ref[per * (j - 3) + m], :, 3 * QCOL :
                ].astype(F32)

        grad = grad_s[...]
        new_w, new_m, new_v = adamw(w_ref[...], grad, m_ref[...], v_ref[...], DECAY)
        g_out[...] = grad
        w_out[...] = new_w
        m_out[...] = new_m
        v_out[...] = new_v

    slab = pl.BlockSpec((part, wide), lambda j, at: (at[RANKS], j))
    held = [] if before is None else list(before)
    return pl.pallas_call(
        kernel,
        grid_spec=pltpu.PrefetchScalarGridSpec(
            num_scalar_prefetch=1,
            grid=(steps,),
            in_specs=[slab] * 3
            + [pl.BlockSpec((RANKS, part, PROJ), lambda j, at: (0, 0, 0))]
            + [pl.BlockSpec(memory_space=pl.ANY)] * len(held),
            out_specs=[slab] * 4,
            scratch_shapes=[pltpu.VMEM((part, wide), F32)],
        ),
        out_shape=[jax.ShapeDtypeStruct((rows, cols), F32)] * 4,
        input_output_aliases={5 + i: i for i in range(len(held))},
        cost_estimate=pl.CostEstimate(
            flops=20 * part * cols, bytes_accessed=30 * part * cols, transcendentals=part * cols
        ),
        name="adamw_rows",
    )(slots, weight, first, second, grads, *held)


def make_on_device(mesh):
    shards = mesh.shape["shard"]
    copies = mesh.shape["replica"]
    fold = shards // RANKS
    rank_of = lambda z, y, c: (z * 2 + y) * 2 + c

    def moves(target):
        pairs = []
        for z in range(NZ):
            for y in range(2):
                for c in range(2):
                    to = rank_of(*target(z, y, c))
                    for f in range(fold):
                        pairs.append((rank_of(z, y, c) * fold + f, to * fold + f))
        return pairs

    swap_core = moves(lambda z, y, c: (z, y, 1 - c))
    swap_y = moves(lambda z, y, c: (z, 1 - y, c))
    up_z = [moves(lambda z, y, c, n=n: ((z + n) % NZ, y, c)) for n in range(NZ)]

    def core(x):
        return lax.ppermute(x, "shard", swap_core)

    def across_y(x):
        return lax.ppermute(x, "shard", swap_y)

    def along_z(x, n):
        return lax.ppermute(x, "shard", up_z[n % NZ])

    def across_fold(x, n):
        return lax.ppermute(
            x,
            "shard",
            [(r * fold + f, r * fold + (f + n) % fold) for r in range(RANKS) for f in range(fold)],
        )

    def next_copy(x, n):
        return lax.ppermute(x, "replica", [(i, (i + n) % copies) for i in range(copies)])

    def fold_gather(x, f):
        if fold == 1:
            return x
        parts = jnp.stack([x] + [across_fold(x, n) for n in range(1, fold)])
        order = (f - jnp.arange(fold)) % fold
        return jnp.take(parts, order, axis=0).reshape((fold * x.shape[0],) + x.shape[1:])

    def fold_scatter(x, f):
        if fold == 1:
            return x
        parts = x.reshape((fold, x.shape[0] // fold) + x.shape[1:])
        total = lax.dynamic_index_in_dim(parts, f, 0, keepdims=False)
        for n in range(1, fold):
            part = lax.dynamic_index_in_dim(parts, (f + n) % fold, 0, keepdims=False)
            total = total + across_fold(part, n).astype(F32)
        return total

    def gather_z(x):
        above = along_z(x, 3)
        below = along_z(x, 1)
        opposite = along_z(above, 3)
        chunks = []
        for x in (x, below, opposite, above):
            flipped = across_y(x)
            far = core(x)
            chunks.append((x, flipped, far, core(flipped)))
        return chunks

    def table(me, entries):
        rows = [
            entries(r // 4, r // 2 % 2, r % 2) for r in range(RANKS) for _ in range(fold)
        ]
        return lax.dynamic_index_in_dim(jnp.array(rows, dtype=jnp.int32), me, 0, keepdims=False)

    def near(z, y, c, n, dy, dc):
        return rank_of((z + n) % NZ, (y + dy) % 2, (c + dc) % 2)

    def columns_of(w_in, me, z, y, c, f, copy):
        rows = w_in.shape[0] * fold
        part = rows // copies
        if fold == 1 and copies == 2:
            def slots(z, y, c):
                order = [near(z, y, c, n, i, j) for j in (0, 1) for n in range(NZ) for i in (0, 1)]
                return [order.index(r) for r in range(RANKS)]

            place = jnp.concatenate([table(me, slots), copy.reshape(1)])
            *kept, sent = ranks_first(w_in, place, part)
            came = core(sent).reshape(NZ, 2, part, PROJ)
            pieces = []
            for n in (0, 2, 1, 3):
                piece = jnp.stack([kept[n], came[n]], axis=1)
                if n:
                    piece = along_z(piece, n)
                over = across_y(piece[1])
                piece = jnp.concatenate([piece[0], over])
                pieces.append((piece, next_copy(piece, 1)))
            home = table(
                me,
                lambda z, y, c: [
                    2 * near(z, y, c, -n, i, j) for n in (0, 2, 1, 3) for i in (0, 1) for j in (0, 1)
                ],
            )
            home = jnp.concatenate([home + copy, home + (1 - copy)])
            return rows_home([p[0] for p in pieces] + [p[1] for p in pieces], home, part)
        low_in = fold_gather(w_in.astype(LOW), f)
        by_rank = jnp.concatenate(
            [
                low_in[:, :D].reshape(rows, RANKS, QCOL),
                low_in[:, D : 2 * D].reshape(rows, RANKS, QCOL),
                low_in[:, 2 * D : 3 * D].reshape(rows, RANKS, QCOL),
                low_in[:, 3 * D :].reshape(rows, RANKS, FCOL),
            ],
            axis=2,
        )
        turned = by_rank.transpose(1, 0, 2).reshape(NZ, 2, 2, rows, PROJ)
        return to_ranks(turned, z, y, c).reshape(D, PROJ)

    def to_ranks(blocks, z, y, c):
        kept = lax.dynamic_index_in_dim(blocks, c, 2, keepdims=False)
        came = core(lax.dynamic_index_in_dim(blocks, 1 - c, 2, keepdims=False))
        blocks = jnp.stack([jnp.where(c == 0, kept, came), jnp.where(c == 0, came, kept)], axis=2)
        kept = lax.dynamic_index_in_dim(blocks, y, 1, keepdims=False)
        came = across_y(lax.dynamic_index_in_dim(blocks, 1 - y, 1, keepdims=False))
        blocks = jnp.stack([jnp.where(y == 0, kept, came), jnp.where(y == 0, came, kept)], axis=1)
        by_z = [lax.dynamic_index_in_dim(blocks, z, 0, keepdims=False)]
        for n in range(1, NZ):
            by_z.append(
                along_z(lax.dynamic_index_in_dim(blocks, (z + n) % NZ, 0, keepdims=False), n)
            )
        return jnp.take(jnp.stack(by_z), (z - jnp.arange(NZ)) % NZ, axis=0)

    def start_in(grad_in, me, copy):
        part = D // RANKS // 2
        place = table(
            me,
            lambda z, y, c: [(z + n) % NZ for n in GRAD_ORDER]
            + [near(0, y, c, 0, i, j) for i in (0, 1) for j in (0, 1)],
        )
        place = jnp.concatenate([place, copy.reshape(1)])
        sent, kept = split_sum(grad_in, (), place, part, 0, NZ, F32)
        return place, kept, next_copy(sent, 1)

    def finish_in(grad_in, early, w_in, m_in, v_in, me, z, y, c, f, copy):
        rows = w_in.shape[0] * fold
        part = rows // copies
        if fold == 1 and copies == 2:
            place, kept, heard = early
            halves = []
            for i, n in enumerate(GRAD_ORDER):
                sent, base = split_sum(
                    grad_in[EARLY:], (kept, heard), place, part, i, 1, LOW
                )
                late = next_copy(sent, 1)
                block = (base + late).astype(LOW)
                if n:
                    block = along_z(block, n)
                came = across_y(block[2:])
                block = jnp.stack([block[:2], came])
                came = core(block[:, 1])
                block = jnp.stack([block[:, 0], came], axis=1)
                block = block.reshape(4, part, PROJ)
                came = next_copy(block, 1)
                halves.append((block, came))
            own = jnp.concatenate([h[0] for h in halves])
            other = jnp.concatenate([h[1] for h in halves])

            def slots(z, y, c):
                order = [near(z, y, c, -n, i, j) for n in GRAD_ORDER for i in (0, 1) for j in (0, 1)]
                return [order.index(r) for r in range(RANKS)]

            slot = table(me, slots)
            mine = jnp.concatenate([slot, copy.reshape(1)])
            theirs = jnp.concatenate([slot, 1 - copy.reshape(1)])
            first = adamw_rows(w_in, m_in, v_in, own, mine)
            return adamw_rows(w_in, m_in, v_in, other, theirs, first)
        grad_in = sum(grad_in[1:], grad_in[0])
        back = to_ranks(grad_in.astype(LOW).reshape(NZ, 2, 2, rows, PROJ), z, y, c)
        both = back.reshape(RANKS, rows, PROJ).transpose(1, 0, 2)
        both = jnp.concatenate(
            [
                both[:, :, :QCOL].reshape(rows, D),
                both[:, :, QCOL : 2 * QCOL].reshape(rows, D),
                both[:, :, 2 * QCOL : 3 * QCOL].reshape(rows, D),
                both[:, :, 3 * QCOL :].reshape(rows, FF),
            ],
            axis=1,
        )
        grad = fold_scatter(both, f).astype(F32)
        for moved in [next_copy(grad, n) for n in range(1, copies)]:
            grad = grad + moved
        return (grad,) + adamw(w_in, grad, m_in, v_in, DECAY)

    def on_device(
        tokens,
        seg_ids,
        cotangent,
        w_in,
        w_out,
        w_fc2,
        vectors,
        m_in,
        v_in,
        m_out,
        v_out,
        m_fc2,
        v_fc2,
        m_vec,
        v_vec,
    ):
        length = tokens.shape[0]
        me = lax.axis_index("shard")
        copy = lax.axis_index("replica")
        t = me // fold
        f = me % fold
        z, y, c = t // 4, (t // 2) % 2, t % 2

        g_chunks = gather_z(cotangent)

        w_cols = columns_of(w_in, me, z, y, c, f, copy)
        w_pair = jnp.concatenate(
            [fold_gather(w_out.astype(LOW), f), fold_gather(w_fc2.astype(LOW), f)], axis=0
        )

        order = jnp.arange(length, dtype=jnp.int32)
        same = seg_ids[:, None] == seg_ids[None, :]
        place = jnp.sum((same & (order[None, :] < order[:, None])).astype(F32), axis=1)
        grouped = fold_gather(vectors.reshape(-1, 11), f)
        small = jnp.concatenate([grouped[:, 9], grouped[:, 10], seg_ids.astype(F32), place])
        small = small.reshape(1, -1)
        heard = [small]
        for n in range(1, NZ):
            heard.append(along_z(small, n))
        small = jnp.concatenate(heard, axis=0)
        small = jnp.stack([small, across_y(small)], axis=1)
        small = jnp.stack([small, core(small)], axis=2)
        gains = small[..., : 2 * QCOL]
        gains = jnp.take(gains, (z - jnp.arange(NZ)) % NZ, axis=0)
        gains = jnp.where(y == 0, gains, gains[:, ::-1])
        gains = jnp.where(c == 0, gains, gains[:, :, ::-1]).reshape(RANKS, 2, QCOL)
        gain = gains[:, 0].reshape(D)
        shift = gains[:, 1].reshape(D)
        tail = small[..., 2 * QCOL :].transpose(0, 2, 1, 3).reshape(NZ, 4, 2, length)
        segs = tail[:, :, 0]
        places = tail[:, :, 1]
        lane = jnp.arange(QCOL, dtype=jnp.int32) % HEAD
        freqs = 10000.0 ** (-(lane % (ROT // 2)).astype(F32) * (2.0 / ROT))
        freqs = jnp.where(lane < ROT, freqs, 0.0)
        inputs = tokens.astype(F32)
        centred = inputs - jnp.mean(inputs, axis=1, keepdims=True)
        inv_std = lax.rsqrt(jnp.mean(centred * centred, axis=1, keepdims=True) + NORM_EPS)
        standard = centred * inv_std
        normed = (standard * gain + shift).astype(LOW)
        n_chunks = gather_z(normed)

        bias_in = jnp.concatenate(
            [grouped[:, 0], grouped[:, 1], grouped[:, 2], grouped[:, 3:7].reshape(FCOL)]
        ).reshape(1, PROJ)
        bias_tail = lax.dynamic_update_slice(
            jnp.zeros((D,), F32), grouped[:, 7] + grouped[:, 8], (t * QCOL,)
        )

        def scatter_add(near, far, n, carried):
            came = core(far)
            sent = (near[:, length:] + came[:, length:].astype(F32)).astype(LOW)
            over = across_y(sent)
            own = near[:, :length] + came[:, :length].astype(F32) + over.astype(F32)
            if carried is not None:
                own = own + carried.astype(F32)
            if n == 0:
                return own
            return along_z(own.astype(LOW), 1 if n == 3 else 3)

        totals = []
        early = None
        grad_in = []
        grad_pair = []
        proj_sum = []
        for n in CHUNKS:
            gc = g_chunks[n]
            nc = n_chunks[n]
            if grad_in:
                gc, nc, grad_in[-1] = lax.optimization_barrier((gc, nc, grad_in[-1]))
            angles = places[n].reshape(4 * length, 1) * freqs
            cosine = jnp.cos(angles)
            sine = jnp.sin(angles)
            n_cat, g_cat, ah, gp, far, near, sums = run_chunk(
                nc,
                gc,
                w_cols,
                w_pair,
                bias_in,
                bias_tail.reshape(1, D),
                cosine,
                sine,
                segs[n].reshape(4 * length, 1),
                segs[n].reshape(4, 1, length),
            )
            grad_in.append(dot(n_cat, gp, BY_FIRST))
            grad_pair.append(dot(ah, g_cat, BY_FIRST))
            proj_sum.append(sums)
            carried = scatter_add(near, far, n, totals.pop() if n == 1 else None)
            totals.append(carried)
            if len(grad_in) == EARLY and fold == 1 and copies == 2:
                early = start_in(grad_in, me, copy)
        gn_total = sum([part[0].astype(F32) for part in totals[1:]], totals[0][0])
        out_total = sum([part[1].astype(F32) for part in totals[1:]], totals[0][1])
        proj_sum = sum(proj_sum[1:], proj_sum[0])
        grad_pair = sum(grad_pair[1:], grad_pair[0])

        output = (inputs + out_total).astype(LOW)
        upstream = cotangent.astype(F32)
        scaled = gn_total * gain
        grad_tokens = upstream + inv_std * (
            scaled
            - jnp.mean(scaled, axis=1, keepdims=True)
            - standard * jnp.mean(scaled * standard, axis=1, keepdims=True)
        )

        sums = jnp.stack(
            [jnp.sum(upstream, axis=0), jnp.sum(gn_total * standard, axis=0), jnp.sum(gn_total, axis=0)]
        )
        sums = sums + core(sums)
        sums = sums + across_y(sums)
        for moved in [along_z(sums, n) for n in range(1, NZ)]:
            sums = sums + moved
        sums = lax.dynamic_slice(sums, (0, t * QCOL), (3, QCOL))
        vec = jnp.concatenate(
            [
                proj_sum[0, : 3 * QCOL].reshape(3, QCOL).T,
                proj_sum[0, 3 * QCOL :].reshape(QCOL, 4),
                sums[0][:, None],
                sums[0][:, None],
                sums[1][:, None],
                sums[2][:, None],
            ],
            axis=1,
        )
        vec = fold_scatter(vec, f).reshape(-1)
        for moved in [next_copy(vec, n) for n in range(1, copies)]:
            vec = vec + moved

        g_out = fold_scatter(grad_pair[:QCOL], f)
        g_fc2 = fold_scatter(grad_pair[QCOL:], f)
        g_pair = jnp.concatenate([g_out, g_fc2], axis=0).astype(LOW)
        pair_total = g_pair.astype(F32)
        for n in range(1, copies):
            pair_total = pair_total + next_copy(g_pair, n).astype(F32)
        grad_out = pair_total[: g_out.shape[0]]
        grad_fc2 = pair_total[g_out.shape[0] :]

        grad_w_in, new_in, new_m_in, new_v_in = finish_in(
            grad_in, early, w_in, m_in, v_in, me, z, y, c, f, copy
        )
        new_out, new_m_out, new_v_out = adamw(w_out, grad_out, m_out, v_out, DECAY)
        new_fc2, new_m_fc2, new_v_fc2 = adamw(w_fc2, grad_fc2, m_fc2, v_fc2, DECAY)
        new_vec, new_m_vec, new_v_vec = adamw(vectors, vec, m_vec, v_vec, 0.0)
        return (
            output,
            grad_tokens,
            grad_w_in,
            grad_out,
            grad_fc2,
            vec,
            new_in,
            new_out,
            new_fc2,
            new_vec,
            new_m_in,
            new_v_in,
            new_m_out,
            new_v_out,
            new_m_fc2,
            new_v_fc2,
            new_m_vec,
            new_v_vec,
        )

    return on_device


def solution(mesh):
    both = P(("replica", "shard"), None)
    flat = P("shard")
    rows = P("shard", None)
    return jax.shard_map(
        make_on_device(mesh),
        mesh=mesh,
        in_specs=(both, P(("replica", "shard")), both, rows, rows, rows, flat)
        + (rows,) * 6
        + (flat, flat),
        out_specs=(both, both, rows, rows, rows, flat)
        + (rows, rows, rows, flat)
        + (rows,) * 6
        + (flat, flat),
        check_vma=False,
    )
```
